128 devices in a mesh: tm: 4 (over z), chan: 32 (over x, y, core).
Axes of the slice: x: 4, y: 4, z: 4, core: 2. Of those that a mesh axis runs over, the one named last changes fastest.
Arguments:
- phase_step: float32 [8, 256, 131072], P(None, 'tm', 'chan'), may hold values from -3.1416 to 3.1416, as said below
- wrap_count: int32 [8, 256, 131072], P(None, 'tm', 'chan'), may hold values from -1 to 1
- coupling: float32 [8], replicated, may hold values from 0.5 to 2
- filter_taps: float32 [8, 128], replicated, may hold values from -0.06 to 0.06
Outputs:
- strain: float32 [8, 256, 131072], P(None, 'tm', 'chan')
The draws below stay inside these ranges and needn't reach their ends.
Inputs may be any that keep to these rules, and one draw needn't show every extreme that they name: `phase_step`: wrapped phase differences, within -pi to pi.
All inputs are finite; a program needn't handle non-finite values.
Results may differ from the reference program's by a relative error of at most 0.00007.
Values sent between devices are 32-bit elements; how exact they have to be, the bound alone decides.
A program may use at most 128 MiB of HBM per device.

```python
import math
import jax
import jax.numpy as jnp
from jax import lax

CABLES = 8
TAPS = 128
CHANNELS = 131072
TIME = 256


def draw_phase_step(key, part):
    first_key = jax.random.fold_in(key, 11)
    second_key = jax.random.fold_in(key, 23)
    channel_ramp = 1.0 + 2.0 * jnp.arange(CHANNELS, dtype=jnp.float32) / (CHANNELS - 1)
    common = jax.random.uniform(first_key, (1, TIME, 1), jnp.float32, -0.7, 0.7)
    noise = jax.random.uniform(second_key, (CABLES, TIME, CHANNELS), jnp.float32, -1.0, 1.0)
    return common * channel_ramp[None, None, :] + noise


def set_ends(drawn, stream_key, low, top_value):
    longest = drawn.shape.index(max(drawn.shape))
    spots = []
    for shift in (0, 1):
        where = [jax.random.randint(jax.random.fold_in(stream_key, axis), (), 0, length) for axis, length in enumerate(drawn.shape)]
        where[longest] = (where[longest] + shift) % drawn.shape[longest]
        spots.append(tuple(where))
    return drawn.at[spots[0]].set(low).at[spots[1]].set(top_value)


def normal_values(own_key, extent, scale, bound, kind=jnp.bfloat16):
    values = scale * jax.random.normal(own_key, extent, jnp.float32)
    return jnp.clip(values, min=-bound, max=bound).astype(kind)


def setup_inputs(seed: int = 0) -> dict:
    seeds = jax.random.split(jax.random.key(seed), 5)
    return {
        "phase_step": draw_phase_step(jax.random.fold_in(seeds[4], 71), 0),
        "wrap_count": set_ends(jax.random.randint(seeds[1], (CABLES, TIME, CHANNELS), -1, 2), jax.random.fold_in(seeds[1], 1), -1, 1).astype(jnp.int32),
        "coupling": jnp.clip(jnp.exp(jax.random.uniform(seeds[2], (CABLES,), jnp.float32, math.log(0.5), math.log(2.0))), 0.5, 2.0),
        "filter_taps": normal_values(seeds[3], (CABLES, TAPS), 0.01, 0.06, jnp.float32),
    }


two_pi = 2.0 * math.pi


def spatial_filter(padded, filter_taps):
    stacked = jnp.transpose(padded, (1, 0, 2))
    kernel = filter_taps[:, None, :]
    result = lax.conv_general_dilated(stacked, kernel, (1,), "VALID", feature_group_count=filter_taps.shape[0], precision=lax.Precision.HIGHEST)
    return jnp.transpose(result, (1, 0, 2))


def reference(phase_step, wrap_count, coupling, filter_taps):
    increment = phase_step + two_pi * wrap_count.astype(jnp.float32)
    unwrapped = jnp.cumsum(increment, axis=1)
    population = phase_step.shape[0] * phase_step.shape[2]
    common = jnp.sum(unwrapped, axis=(0, 2)) / population
    leveled = unwrapped - coupling[:, None, None] * common[None, :, None]
    half = TAPS // 2
    padded = jnp.pad(leveled, ((0, 0), (0, 0), (half, half - 1)))
    filtered = spatial_filter(padded, filter_taps)
    return (leveled - filtered) * (1.0 / (4.0 * two_pi))
```

```python
import functools
import math

import jax
import jax.numpy as jnp
from jax import lax
from jax.experimental import pallas as pl
from jax.experimental.pallas import tpu as pltpu
from jax.sharding import PartitionSpec as P

two_pi = 2.0 * math.pi
scale = 1.0 / (4.0 * two_pi)
LANES = 128
GROUP = 8
f32 = jnp.float32
bf16 = jnp.bfloat16


def halves(x):
    high = x.astype(bf16)
    return high, (x - high.astype(f32)).astype(bf16)


def running_sum(rows, sublane):
    for shift in (1, 2, 4):
        turned = [pltpu.roll(row, shift, 0) for row in rows]
        wraps = sublane < shift
        summed = []
        for i, row in enumerate(rows):
            above = turned[i - 1] if i else jnp.zeros_like(row)
            summed.append(row + jnp.where(wraps, above, turned[i]))
        rows = summed
    for i in range(1, len(rows)):
        rows[i] = rows[i] + rows[i - 1]
    return rows


def main_kernel(
    n_tm, n_chan,
    phase, wrap, coupling, taps,
    y_hbm, offset_out, edge_out, common_out,
    pbuf, wbuf, zhi, zlo, ybuf, matrix, sums, ends,
    send_left, send_right, halo_left, halo_right,
    ends_in, far_send, far_in, own_row, row_in, plane_row, plane_in,
    sem_in, sem_out, sem_edge,
    s_left, s_right, r_left, r_right,
    s_ends, r_ends, s_far, r_far, s_row, r_row, s_plane, r_plane,
):
    cables, times, width = phase.shape
    blocks = width // LANES
    groups = blocks // GROUP
    parts = times // 16
    tm = lax.axis_index("tm")
    chan = lax.axis_index("chan")

    def load(c):
        return (
            pltpu.make_async_copy(phase.at[c], pbuf.at[c], sem_in.at[0, c]),
            pltpu.make_async_copy(wrap.at[c], wbuf.at[c], sem_in.at[1, c]),
        )

    for c in range(cables):
        for copy in load(c):
            copy.start()

    barrier = pltpu.get_barrier_semaphore()

    @pl.loop(1, n_chan)
    def _(d):
        pl.semaphore_signal(barrier, inc=1, device_id={"chan": lax.rem(chan + d, n_chan)})

    for d in range(1, n_tm):
        pl.semaphore_signal(barrier, inc=1, device_id={"tm": lax.rem(tm + d, n_tm)})

    lane = lax.broadcasted_iota(jnp.int32, (1, 2 * LANES), 1)

    @pl.loop(0, cables)
    def _(c):
        row = (jnp.where(lane == LANES // 2, 1.0, 0.0) - taps[c]) * scale
        row = jnp.where(lane < LANES, row, 0.0)
        high = row.astype(bf16).astype(f32)
        for i, part in enumerate((high, row - high)):
            spread = jnp.broadcast_to(part, (LANES, 2 * LANES))
            turned = pltpu.roll(spread, 0, 1, stride=1, stride_axis=0)
            matrix[c, :, i * LANES : (i + 1) * LANES] = turned.T.astype(bf16)

    sublane = lax.broadcasted_iota(jnp.int32, (8, LANES), 0)
    sums[...] = jnp.zeros_like(sums)

    @pl.when(chan == 0)
    def _():
        halo_left[...] = jnp.zeros_like(halo_left)

    @pl.when(chan == n_chan - 1)
    def _():
        halo_right[...] = jnp.zeros_like(halo_right)

    pl.semaphore_wait(barrier, n_chan - 1 + n_tm - 1)

    def to_left(c):
        return pltpu.make_async_remote_copy(
            send_left.at[c], halo_right.at[c], s_left.at[c], r_right.at[c],
            device_id={"chan": chan - 1},
        )

    def to_right(c):
        return pltpu.make_async_remote_copy(
            send_right.at[c], halo_left.at[c], s_right.at[c], r_left.at[c],
            device_id={"chan": chan + 1},
        )

    def later(d, src, dst, send, recv):
        return pltpu.make_async_remote_copy(
            src, dst, send, recv, device_id={"tm": tm + d}
        )

    def ends_to(d, c):
        return later(d, ends.at[c], ends_in.at[tm, c], s_ends.at[d - 1, c], r_ends.at[d - 1, c])

    def far_to(d):
        return later(d, far_send, far_in.at[tm], s_far.at[d - 1], r_far.at[d - 1])

    def row_to(d):
        return later(d, own_row, row_in.at[tm], s_row.at[d - 1], r_row.at[d - 1])

    def for_later(action):
        for d in range(1, n_tm):
            pl.when(tm + d < n_tm)(functools.partial(action, d))

    def from_earlier(action):
        for d in range(1, n_tm):
            pl.when(tm - d >= 0)(functools.partial(action, d))

    def accumulate(c, g):
        total = [None] * (times // 8)
        for b in range(GROUP):
            block = g * GROUP + b
            col = pl.multiple_of(block * LANES, LANES)
            rows = []
            for i in range(times // 8):
                step = pbuf[c, 8 * i : 8 * i + 8, pl.ds(col, LANES)]
                turns = wbuf[c, 8 * i : 8 * i + 8, pl.ds(col, LANES)]
                rows.append(step + two_pi * turns.astype(f32))
            rows = running_sum(rows, sublane)
            for i, row in enumerate(rows):
                total[i] = row if total[i] is None else total[i] + row
            ends[c, pl.ds(block, 1), :] = rows[-1][7:8, :]
            if b == 0:
                slot = jnp.where(g == 0, c, cables)
                for i, row in enumerate(rows):
                    send_left[slot, 8 * i : 8 * i + 8, :] = row
            if b == GROUP - 1:
                slot = jnp.where(g == groups - 1, c, cables)
                for i, row in enumerate(rows):
                    send_right[slot, 8 * i : 8 * i + 8, :] = row
            for i in range(parts):
                x = jnp.concatenate(rows[2 * i : 2 * i + 2], axis=0)
                high, low = halves(x)
                zhi[c, i, block + 1] = high
                zlo[c, i, block + 1] = low
        for i, row in enumerate(total):
            sums[8 * i : 8 * i + 8, :] += row

    @pl.loop(0, cables)
    def _(c):
        for copy in load(c):
            copy.wait()

        @pl.loop(0, groups)
        def _(g):
            accumulate(c, g)

        @pl.when(chan > 0)
        def _():
            to_left(c).start()

        @pl.when(chan < n_chan - 1)
        def _():
            to_right(c).start()

        for_later(lambda d: ends_to(d, c).start())

    both = jnp.concatenate([sums[...], jnp.zeros_like(sums)], axis=0)
    own_row[...] = jnp.sum(both.T, axis=0, keepdims=True)
    for_later(lambda d: row_to(d).start())

    def window(z, c, w):
        return jnp.concatenate(
            [jnp.concatenate([z[c, i, w], z[c, i, w + 1]], axis=1) for i in range(parts)],
            axis=0,
        )

    def push(c):
        for mxu in range(2):
            pltpu.matmul_push_rhs(matrix[c], 0, mxu)

    def joined(pair):
        return pair[:, :LANES] + pair[:, LANES:]

    def interior(c, g):
        def body(*acc):
            push(c)
            for b in range(GROUP):
                w = g * GROUP + b
                pltpu.matmul_acc_lhs(acc[b], window(zhi, c, w), 0 if b < 2 else None)
                pltpu.matmul_acc_lhs(acc[b], window(zlo, c, w))
            for b in range(GROUP):
                col = pl.multiple_of((g * GROUP + b) * LANES, LANES)
                ybuf[c, :, pl.ds(col, LANES)] = joined(pltpu.matmul_pop(acc[b]))

        pl.run_scoped(body, *[pltpu.ACC(b % 2)((times, 2 * LANES), f32) for b in range(GROUP)])

    def middle_out(c):
        return pltpu.make_async_copy(
            ybuf.at[c, :, pl.ds(LANES, width - LANES)],
            y_hbm.at[c, :, pl.ds(LANES, width - LANES)],
            sem_out.at[c],
        )

    def edges_out(c):
        return [
            pltpu.make_async_copy(
                ybuf.at[c, :, pl.ds(col, LANES)], y_hbm.at[c, :, pl.ds(col, LANES)], sem_edge.at[i, c]
            )
            for i, col in enumerate((0, width))
        ]

    def to_plane(d):
        return pltpu.make_async_remote_copy(
            plane_row, plane_in.at[chan], s_plane.at[d], r_plane.at[d],
            device_id={"chan": lax.rem(chan + d, n_chan)},
        )

    def relay():
        from_earlier(lambda d: row_to(d).wait_recv())
        row = own_row[...]
        for source in range(n_tm - 1):
            last = row_in[source][:, times - 1 : times]
            row = row + jnp.where(source < tm, last, 0.0)
        plane_row[...] = row
        plane_in[chan] = row

        @pl.loop(1, n_chan)
        def _(d):
            to_plane(d).start()

        @pl.when(chan > 0)
        def _():
            @pl.loop(0, cables)
            def _(c):
                to_right(c).wait_recv()

        @pl.when(chan < n_chan - 1)
        def _():
            @pl.loop(0, cables)
            def _(c):
                to_left(c).wait_recv()

        for c in range(cables):
            far_send[c : c + 1, :] = halo_left[c, times - 1 : times, :]
            far_send[cables + c : cables + c + 1, :] = halo_right[c, times - 1 : times, :]
        for_later(lambda d: far_to(d).start())

    @pl.loop(0, cables)
    def _(c):
        pl.when(c == 2)(relay)

        @pl.loop(0, groups)
        def _(g):
            interior(c, g)

        middle_out(c).start()

    @pl.loop(0, cables)
    def _(c):
        from_earlier(lambda d: ends_to(d, c).wait_recv())

    from_earlier(lambda d: far_to(d).wait_recv())
    far = jnp.zeros_like(far_send)
    for source in range(n_tm - 1):
        far = far + jnp.where(source < tm, far_in[source], 0.0)
    far_send_sum = far
    far_rows = far_send_sum

    position = lax.broadcasted_iota(jnp.int32, (48, LANES), 0)
    ones = jnp.ones((16, LANES), f32)
    which = lax.broadcasted_iota(jnp.int32, (16, LANES), 0)
    no_left = jnp.where(which == 1, 0.0, ones).astype(bf16)
    no_right = jnp.where(which == 2, 0.0, ones).astype(bf16)
    one_rows = jnp.concatenate([no_left, no_right], axis=1)

    for c in range(cables):
        for i in range(parts):
            for halo, at in ((halo_left, 0), (halo_right, blocks + 1)):
                high, low = halves(halo[c, 16 * i : 16 * i + 16, :])
                zhi[c, i, at] = high
                zlo[c, i, at] = low
        earlier = jnp.zeros((blocks, LANES), f32)
        for source in range(n_tm - 1):
            earlier = earlier + jnp.where(source < tm, ends_in[source, c], 0.0)
        tail = jnp.zeros((48 - blocks, LANES), f32)
        here = jnp.concatenate([earlier, tail], axis=0)
        before = pltpu.roll(here, 1, 0)
        before = jnp.where(position == 0, far_rows[c : c + 1, :], before)
        here = jnp.where(position == blocks, far_rows[cables + c : cables + c + 1, :], here)

        def body(first, last, small, constant):
            push(c)
            for k, z in enumerate((zhi, zlo)):
                pltpu.matmul_acc_lhs(first, window(z, c, 0), None if k else 0)
                pltpu.matmul_acc_lhs(last, window(z, c, blocks), None if k else 0)
            before_parts, here_parts = halves(before), halves(here)
            for x, y in zip(before_parts, here_parts):
                pltpu.matmul_acc_lhs(small, jnp.concatenate([x, y], axis=1))
            pltpu.matmul_acc_lhs(constant, one_rows)
            ybuf[c, :, 0:LANES] = joined(pltpu.matmul_pop(first))
            ybuf[c, :, width : width + LANES] = joined(pltpu.matmul_pop(last))
            offset_out[c] = joined(pltpu.matmul_pop(small))
            flat = joined(pltpu.matmul_pop(constant))
            flat = flat * coupling[c]
            edge = jnp.broadcast_to(flat[0:1, :], (48, LANES))
            edge = jnp.where((position == 0) & (chan == 0), flat[1:2, :], edge)
            edge = jnp.where((position == blocks) & (chan == n_chan - 1), flat[2:3, :], edge)
            edge_out[c] = edge

        pl.run_scoped(
            body,
            pltpu.ACC(0)((times, 2 * LANES), f32),
            pltpu.ACC(1)((times, 2 * LANES), f32),
            pltpu.ACC(0)((48, 2 * LANES), f32),
            pltpu.ACC(1)((16, 2 * LANES), f32),
        )
        for copy in edges_out(c):
            copy.start()

    @pl.loop(1, n_chan)
    def _(d):
        to_plane(d).wait_recv()

    row = jnp.sum(plane_in[...], axis=0) * (1.0 / (cables * width * n_chan))
    common_out[...] = jnp.broadcast_to(row, (LANES, LANES)).T[:times]

    @pl.loop(1, n_chan)
    def _(d):
        to_plane(d).wait_send()

    for_later(lambda d: row_to(d).wait_send())
    for_later(lambda d: far_to(d).wait_send())

    @pl.loop(0, cables)
    def _(c):
        for_later(lambda d: ends_to(d, c).wait_send())

        @pl.when(chan > 0)
        def _():
            to_left(c).wait_send()

        @pl.when(chan < n_chan - 1)
        def _():
            to_right(c).wait_send()

        middle_out(c).wait()
        for copy in edges_out(c):
            copy.wait()


def final_kernel(y, offset, edge, common, out):
    times = common.shape[0]
    blocks = out.shape[2] // LANES
    left = lax.broadcasted_iota(jnp.int32, (times, LANES), 1) < LANES // 2
    before = None
    for w in range(blocks + 1):
        v = y[0, :, w * LANES : (w + 1) * LANES] + (
            offset[0, w : w + 1, :] - common[...] * edge[0, w : w + 1, :]
        )
        v = pltpu.roll(v, LANES // 2, 1)
        if w:
            out[0, :, (w - 1) * LANES : w * LANES] = jnp.where(left, before, v)
        before = v


def shards(phase_step, wrap_count, coupling, filter_taps):
    cables, times, width = phase_step.shape
    blocks = width // LANES
    n_tm, n_chan = lax.axis_size("tm"), lax.axis_size("chan")
    taps = jnp.pad(filter_taps, ((0, 0), (0, LANES)))[:, None, :]
    vmem, dma = pltpu.VMEM, pltpu.SemaphoreType.DMA
    full = (cables, times, width)
    edge = (cables + 1, times, LANES)
    z = (cables, times // 16, blocks + 2, 16, LANES)
    small = jax.ShapeDtypeStruct((cables, 48, LANES), f32)
    y, offset, edges, common = pl.pallas_call(
        functools.partial(main_kernel, n_tm, n_chan),
        out_shape=(
            jax.ShapeDtypeStruct((cables, times, width + LANES), f32),
            small,
            small,
            jax.ShapeDtypeStruct((times, LANES), f32),
        ),
        in_specs=[
            pl.BlockSpec(memory_space=pl.ANY),
            pl.BlockSpec(memory_space=pl.ANY),
            pl.BlockSpec(memory_space=pltpu.SMEM),
            pl.BlockSpec(memory_space=vmem),
        ],
        out_specs=(
            pl.BlockSpec(memory_space=pl.ANY),
            pl.BlockSpec(memory_space=vmem),
            pl.BlockSpec(memory_space=vmem),
            pl.BlockSpec(memory_space=vmem),
        ),
        scratch_shapes=[
            vmem(full, f32), vmem(full, jnp.int32), vmem(z, bf16), vmem(z, bf16),
            vmem((cables, times, width + LANES), f32),
            vmem((cables, 2 * LANES, 2 * LANES), bf16),
            vmem((times, LANES), f32), vmem((cables, blocks, LANES), f32),
            vmem(edge, f32), vmem(edge, f32),
            vmem((cables, times, LANES), f32), vmem((cables, times, LANES), f32),
            vmem((n_tm, cables, blocks, LANES), f32),
            vmem((2 * cables, LANES), f32), vmem((n_tm, 2 * cables, LANES), f32),
            vmem((1, LANES), f32), vmem((n_tm, 1, LANES), f32),
            vmem((1, LANES), f32), vmem((n_chan, 1, LANES), f32),
            dma((2, cables)), dma((cables,)), dma((2, cables)),
            dma((cables,)), dma((cables,)), dma((cables,)), dma((cables,)),
            dma((n_tm - 1, cables)), dma((n_tm - 1, cables)),
            dma((n_tm - 1,)), dma((n_tm - 1,)),
            dma((n_tm - 1,)), dma((n_tm - 1,)),
            dma((n_chan,)), dma((n_chan,)),
        ],
        compiler_params=pltpu.CompilerParams(
            collective_id=0, has_side_effects=True, vmem_limit_bytes=60 << 20
        ),
        name="level",
    )(phase_step, wrap_count, coupling, taps)
    return pl.pallas_call(
        final_kernel,
        grid=(cables,),
        out_shape=jax.ShapeDtypeStruct(full, f32),
        in_specs=[
            pl.BlockSpec((1, times, width + LANES), lambda c: (c, 0, 0)),
            pl.BlockSpec((1, 48, LANES), lambda c: (c, 0, 0)),
            pl.BlockSpec((1, 48, LANES), lambda c: (c, 0, 0)),
            pl.BlockSpec((times, LANES), lambda c: (0, 0)),
        ],
        out_specs=pl.BlockSpec((1, times, width), lambda c: (c, 0, 0)),
        name="finish",
    )(y, offset, edges, common)


def solution(mesh):
    placed = (P(None, "tm", "chan"), P(None, "tm", "chan"), P(), P())
    return jax.shard_map(
        shards, mesh=mesh, in_specs=placed, out_specs=P(None, "tm", "chan"), check_vma=False
    )
```

```python
import functools
import math

import jax
import jax.numpy as jnp
from jax import lax
from jax.experimental import pallas as pl
from jax.experimental.pallas import tpu as pltpu
from jax.sharding import PartitionSpec as P

two_pi = 2.0 * math.pi
scale = 1.0 / (4.0 * two_pi)
LANES = 128
GROUP = 11
RING = 8
RELAY = 3
LIMIT = 48
f32 = jnp.float32
bf16 = jnp.bfloat16


def halves(x):
    high = x.astype(bf16)
    return high, (x - high.astype(f32)).astype(bf16)


def running_sum(rows, sublane):
    rows = list(rows)
    for k in range(1, len(rows)):
        rows[k] = rows[k] + rows[k - 1]
    before = rows[-1]
    for shift in (1, 2, 4):
        before = before + jnp.where(sublane >= shift, pltpu.roll(before, shift, 0), 0.0)
    before = jnp.where(sublane >= 1, pltpu.roll(before, 1, 0), 0.0)
    return [row + before for row in rows]


def main_kernel(
    n_tm, n_chan,
    phase, wrap, coupling, taps,
    ybuf, offset_out, edge_out, common_out,
    pbuf, wbuf, zhi, zlo, swap_in, swap_out, carry, matrix, sums, ends,
    send_left, send_right, halo_left, halo_right,
    ends_in, far_send, far_in, own_row, row_in, plane_row, plane_in,
    sem_in, s_left, s_right, r_left, r_right,
    s_ends, r_ends, s_far, r_far, s_row, r_row, s_plane, r_plane,
):
    cables, times, width = phase.shape
    blocks = width // LANES
    groups = (blocks + 1) // GROUP
    assert groups * GROUP == blocks + 1 and times == 64
    parts = times // 16
    tm = lax.axis_index("tm")
    chan = lax.axis_index("chan")

    def load(c):
        return (
            pltpu.make_async_copy(phase.at[c], pbuf.at[c, :, pl.ds(0, width)], sem_in.at[0, c]),
            pltpu.make_async_copy(wrap.at[c], wbuf.at[c, :, pl.ds(0, width)], sem_in.at[1, c]),
        )

    for c in range(cables):
        for copy in load(c):
            copy.start()

    barrier = pltpu.get_barrier_semaphore()

    @pl.loop(1, n_chan)
    def _(d):
        pl.semaphore_signal(barrier, inc=1, device_id={"chan": chan ^ d})

    for d in range(1, n_tm):
        pl.semaphore_signal(barrier, inc=1, device_id={"tm": tm ^ d})

    lane = lax.broadcasted_iota(jnp.int32, (1, LANES), 1)

    @pl.loop(0, cables)
    def _(c):
        row = (jnp.where(lane == LANES // 2, 1.0, 0.0) - taps[pl.ds(c, 1), :]) * scale
        row = jnp.concatenate([row, jnp.zeros_like(row)], axis=1)
        high = row.astype(bf16).astype(f32)
        for i, part in enumerate((high, row - high)):
            spread = jnp.broadcast_to(part, (LANES, 2 * LANES))
            turned = pltpu.roll(spread, 0, 1, stride=1, stride_axis=0)
            matrix[c, i * LANES : (i + 1) * LANES, :] = turned.astype(bf16)

    sublane = lax.broadcasted_iota(jnp.int32, (8, LANES), 0)
    left = lax.broadcasted_iota(jnp.int32, (8, LANES), 1) < LANES // 2
    sums[...] = jnp.zeros_like(sums)
    ends[:, blocks:, :] = jnp.zeros((cables, 8, LANES), f32)

    @pl.when(chan == 0)
    def _():
        halo_left[...] = jnp.zeros_like(halo_left)

    @pl.when(chan == n_chan - 1)
    def _():
        halo_right[...] = jnp.zeros_like(halo_right)

    pl.semaphore_wait(barrier, n_chan - 1 + n_tm - 1)

    def to_left(c):
        return pltpu.make_async_remote_copy(
            send_left.at[c], halo_right.at[c], s_left.at[c], r_right.at[c],
            device_id={"chan": chan - 1},
        )

    def to_right(c):
        return pltpu.make_async_remote_copy(
            send_right.at[c], halo_left.at[c], s_right.at[c], r_left.at[c],
            device_id={"chan": chan + 1},
        )

    def later(d, src, dst, send, recv):
        return pltpu.make_async_remote_copy(src, dst, send, recv, device_id={"tm": tm + d})

    def ends_to(d, src, dst):
        return later(d, src, dst, s_ends.at[d - 1], r_ends.at[d - 1])

    def far_to(d):
        return later(d, far_send, far_in.at[tm], s_far.at[d - 1], r_far.at[d - 1])

    def row_to(d):
        return later(d, own_row, row_in.at[tm], s_row.at[d - 1], r_row.at[d - 1])

    def for_later(action):
        for d in range(1, n_tm):
            pl.when(tm + d < n_tm)(functools.partial(action, d))

    def from_earlier(action):
        for d in range(1, n_tm):
            pl.when(tm - d >= 0)(functools.partial(action, d))

    def put(c, at, rows):
        for i in range(parts):
            high, low = halves(jnp.concatenate(rows[2 * i : 2 * i + 2], axis=0))
            zhi[c, i, at] = high
            zlo[c, i, at] = low

    def turn(row):
        return pltpu.roll(row, LANES // 2, 1)

    def accumulate(c, g):
        total = [None] * 8
        final = g == groups - 1
        previous = [jnp.where(g == 0, 0.0, carry[8 * i : 8 * i + 8, :]) for i in range(8)]
        for b in range(GROUP):
            block = g * GROUP + b
            col = pl.ds(pl.multiple_of(block * LANES, LANES), LANES)
            for i in range(8):
                at = slice(8 * i, 8 * i + 8)
                turned = turn(pbuf[c, at, col] + two_pi * wbuf[c, at, col].astype(f32))
                if b == GROUP - 1:
                    turned = jnp.where(final, 0.0, turned)
                swap_in[b][pl.ds(25 * i, 8, stride=3), :] = jnp.where(left, previous[i], turned)
                previous[i] = turned
            rows = running_sum(
                [swap_in[b][pl.ds(3 * k, 8, stride=25), :] for k in range(8)], sublane
            )
            for k, row in enumerate(rows):
                swap_out[b][pl.ds(3 * k, 8, stride=25), :] = row
            rows = [swap_out[b][pl.ds(25 * i, 8, stride=3), :] for i in range(8)]
            for i, row in enumerate(rows):
                total[i] = row if total[i] is None else total[i] + row
            ends[c, pl.ds(block, 1), :] = rows[-1][7:8, :]
            if b == 0:
                slot = jnp.where(g == 0, c, cables)
                for i, row in enumerate(rows):
                    send_left[slot, 8 * i : 8 * i + 8, :] = row
            if b == GROUP - 1:
                slot = jnp.where(final, c, cables)
                for i, row in enumerate(rows):
                    send_right[slot, 8 * i : 8 * i + 8, :] = row
            put(c, block, rows)
        for i, row in enumerate(total):
            sums[8 * i : 8 * i + 8, :] += row
            carry[8 * i : 8 * i + 8, :] = previous[i]

    @pl.loop(0, cables)
    def _(c):
        for copy in load(c):
            copy.wait()

        @pl.loop(0, groups)
        def _(g):
            accumulate(c, g)

        @pl.when(chan > 0)
        def _():
            to_left(c).start()

        @pl.when(chan < n_chan - 1)
        def _():
            to_right(c).start()

        for_later(lambda d: ends_to(d, ends.at[c], ends_in.at[tm, c]).start())

    both = jnp.concatenate([sums[...], jnp.zeros_like(sums)], axis=0)
    own_row[...] = jnp.sum(both.T, axis=0, keepdims=True)
    for_later(lambda d: row_to(d).start())

    def window(z, c, w):
        return jnp.concatenate(
            [jnp.concatenate([z[c, i, w], z[c, i, w + 1]], axis=1) for i in range(parts)],
            axis=0,
        )

    def push(c):
        for mxu in range(2):
            pltpu.matmul_push_rhs(matrix[c], 0, mxu, transpose=True)

    def joined(acc):
        pair = pltpu.matmul_pop(acc)
        return pair[:, :LANES] + pair[:, LANES:]

    def filtered(c, acc):
        push(c)
        order = [*range(1, blocks - 1), 0, blocks - 1]

        def finish(n):
            col = order[n] * LANES
            ybuf[c, :, col : col + LANES] = joined(acc[n % RING])

        for n, w in enumerate(order):
            if n >= RING:
                finish(n - RING)
            pltpu.matmul_acc_lhs(acc[n % RING], window(zhi, c, w), 0 if n < 2 else None)
            pltpu.matmul_acc_lhs(acc[n % RING], window(zlo, c, w))
        for n in range(blocks - RING, blocks):
            finish(n)

    def to_plane(d):
        return pltpu.make_async_remote_copy(
            plane_row, plane_in.at[chan], s_plane, r_plane, device_id={"chan": chan ^ d}
        )

    def all_plane():
        others = plane_in.at[pl.ds(0, n_chan - 1)]
        return pltpu.make_async_remote_copy(
            others, others, s_plane, r_plane, device_id={"chan": chan ^ 1}
        )

    def relay_row():
        from_earlier(lambda d: row_to(d).wait_recv())
        row = own_row[...]
        for source in range(n_tm - 1):
            last = row_in[source][:, times - 1 : times]
            row = row + jnp.where(source < tm, last, 0.0)
        plane_row[...] = row
        plane_in[chan] = row

        @pl.loop(1, n_chan)
        def _(d):
            to_plane(d).start()

    def halos(c):
        @pl.when(chan > 0)
        def _():
            to_right(c).wait_recv()

        @pl.when(chan < n_chan - 1)
        def _():
            to_left(c).wait_recv()

    def relay_far():
        pl.loop(RELAY, cables)(halos)
        inner = left[:1]
        for c in range(cables):
            last = slice(times - 1, times)
            far_send[c : c + 1, :] = jnp.where(inner, halo_left[c, last, :], 0.0)
            far_send[cables + c : cables + c + 1, :] = jnp.where(inner, 0.0, halo_right[c, last, :])
        for_later(lambda d: far_to(d).start())

    @pl.loop(0, cables)
    def _(c):
        @pl.when(c == RELAY)
        def _():
            relay_row()
            relay_far()

        @pl.when(c < RELAY)
        def _():
            halos(c)

        def tile(buffer, i):
            return buffer[c, 8 * i : 8 * i + 8, :]

        for at, low, high in ((0, halo_left, send_left), (blocks, send_right, halo_right)):
            put(c, at, [jnp.where(left, tile(low, i), tile(high, i)) for i in range(8)])
        pl.run_scoped(
            lambda *acc: filtered(c, acc),
            *[pltpu.ACC(n % 2)((times, 2 * LANES), f32) for n in range(RING)],
        )

    from_earlier(lambda d: ends_to(d, ends, ends_in.at[tm]).wait_recv())
    from_earlier(lambda d: far_to(d).wait_recv())
    far = jnp.zeros_like(far_send)
    for source in range(n_tm - 1):
        far = far + jnp.where(source < tm, far_in[source], 0.0)

    padded = blocks + 8
    row_of = lax.broadcasted_iota(jnp.int32, (padded, LANES), 0)
    position = row_of[:blocks]
    ones = jnp.ones((16, LANES), f32)
    which = lax.broadcasted_iota(jnp.int32, (16, LANES), 0)
    half = lax.broadcasted_iota(jnp.int32, (16, LANES), 1) < LANES // 2
    one_rows = jnp.concatenate(
        [
            jnp.where((which == 1) & half, 0.0, ones).astype(bf16),
            jnp.where((which == 2) & ~half, 0.0, ones).astype(bf16),
        ],
        axis=1,
    )

    def constants(*accs):
        for c in range(cables):
            mxu, small, constant = c % 2, accs[2 * c], accs[2 * c + 1]
            here = jnp.zeros((padded, LANES), f32)
            for source in range(n_tm - 1):
                here = here + jnp.where(source < tm, ends_in[source, c], 0.0)
            here = here + jnp.where(row_of == 0, far[c : c + 1, :], 0.0)
            here = here + jnp.where(row_of == blocks, far[cables + c : cables + c + 1, :], 0.0)
            after = pltpu.roll(here, padded - 1, 0)[:blocks]
            pltpu.matmul_push_rhs(matrix[c], 0, mxu, transpose=True)
            for i, pair in enumerate(zip(halves(here[:blocks]), halves(after))):
                pltpu.matmul_acc_lhs(small, jnp.concatenate(pair, axis=1), None if i else 0)
            pltpu.matmul_acc_lhs(constant, one_rows)
        for c in range(cables):
            offset_out[c] = joined(accs[2 * c])
            flat = joined(accs[2 * c + 1]) * coupling[c]
            edge = jnp.broadcast_to(flat[0:1, :], (blocks, LANES))
            edge = jnp.where((position == 0) & (chan == 0), flat[1:2, :], edge)
            edge = jnp.where((position == blocks - 1) & (chan == n_chan - 1), flat[2:3, :], edge)
            edge_out[c] = edge

    pl.run_scoped(
        constants,
        *[
            pltpu.ACC(c % 2)((size, 2 * LANES), f32)
            for c in range(cables)
            for size in (blocks, 16)
        ],
    )

    for_later(lambda d: row_to(d).wait_send())
    for_later(lambda d: far_to(d).wait_send())
    for_later(lambda d: ends_to(d, ends, ends_in.at[tm]).wait_send())

    @pl.loop(0, cables)
    def _(c):
        @pl.when(chan > 0)
        def _():
            to_left(c).wait_send()

        @pl.when(chan < n_chan - 1)
        def _():
            to_right(c).wait_send()

    all_plane().wait_send()
    all_plane().wait_recv()
    row = jnp.sum(plane_in[...], axis=0) * (1.0 / (cables * blocks * LANES * n_chan))
    common_out[...] = jnp.broadcast_to(row, (LANES, LANES)).T[:times]


def final_kernel(y, offset, edge, common, out):
    c = pl.program_id(0)
    mode = common[...]
    for j in range(out.shape[2] // LANES):
        col = slice(j * LANES, (j + 1) * LANES)
        shift = offset[c, j : j + 1, :] - mode * edge[c, j : j + 1, :]
        out[0, :, col] = y[c, :, col] + shift


def shards(phase_step, wrap_count, coupling, filter_taps):
    cables, times, width = phase_step.shape
    blocks = width // LANES
    n_tm, n_chan = lax.axis_size("tm"), lax.axis_size("chan")
    vmem, dma = pltpu.VMEM, pltpu.SemaphoreType.DMA
    full = (cables, times, width)
    wide = (cables, times, width + LANES)
    edge = (cables + 1, times, LANES)
    z = (cables, times // 16, blocks + 1, 16, LANES)
    small = vmem((cables, blocks, LANES), f32)
    leveled = pl.pallas_call(
        functools.partial(main_kernel, n_tm, n_chan),
        out_shape=(
            vmem(full, f32),
            small,
            small,
            vmem((times, LANES), f32),
        ),
        in_specs=[
            pl.BlockSpec(memory_space=pl.ANY),
            pl.BlockSpec(memory_space=pl.ANY),
            pl.BlockSpec(memory_space=pltpu.SMEM),
            pl.BlockSpec(memory_space=vmem),
        ],
        out_specs=(
            pl.BlockSpec(memory_space=vmem),
            pl.BlockSpec(memory_space=vmem),
            pl.BlockSpec(memory_space=vmem),
            pl.BlockSpec(memory_space=vmem),
        ),
        scratch_shapes=[
            vmem(wide, f32), vmem(wide, jnp.int32), vmem(z, bf16), vmem(z, bf16),
            [vmem((200, LANES), f32)] * GROUP, [vmem((200, LANES), f32)] * GROUP, vmem((times, LANES), f32),
            vmem((cables, 2 * LANES, 2 * LANES), bf16),
            vmem((times, LANES), f32), vmem((cables, blocks + 8, LANES), f32),
            vmem(edge, f32), vmem(edge, f32),
            vmem((cables, times, LANES), f32), vmem((cables, times, LANES), f32),
            vmem((n_tm, cables, blocks + 8, LANES), f32),
            vmem((2 * cables, LANES), f32), vmem((n_tm, 2 * cables, LANES), f32),
            vmem((1, LANES), f32), vmem((n_tm, 1, LANES), f32),
            vmem((1, LANES), f32), vmem((n_chan, 1, LANES), f32),
            dma((2, cables)), dma((cables,)), dma((cables,)), dma((cables,)), dma((cables,)),
            dma((n_tm - 1,)), dma((n_tm - 1,)),
            dma((n_tm - 1,)), dma((n_tm - 1,)),
            dma((n_tm - 1,)), dma((n_tm - 1,)),
            dma, dma,
        ],
        compiler_params=pltpu.CompilerParams(
            collective_id=0, has_side_effects=True, vmem_limit_bytes=LIMIT << 20
        ),
        name="level",
    )(phase_step, wrap_count, coupling, filter_taps)
    return pl.pallas_call(
        final_kernel,
        grid=(cables,),
        out_shape=jax.ShapeDtypeStruct(full, f32),
        in_specs=[pl.BlockSpec(memory_space=vmem)] * 4,
        out_specs=pl.BlockSpec((1, times, width), lambda c: (c, 0, 0)),
        compiler_params=pltpu.CompilerParams(vmem_limit_bytes=16 << 20),
        name="finish",
    )(*[pltpu.with_memory_space_constraint(x, vmem) for x in leveled])


def solution(mesh):
    placed = (P(None, "tm", "chan"), P(None, "tm", "chan"), P(), P())
    return jax.shard_map(
        shards, mesh=mesh, in_specs=placed, out_specs=P(None, "tm", "chan"), check_vma=False
    )
```

```python
import functools
import math

import jax
import jax.numpy as jnp
from jax import lax
from jax.experimental import pallas as pl
from jax.experimental.pallas import tpu as pltpu
from jax.sharding import PartitionSpec as P

two_pi = 2.0 * math.pi
scale = 1.0 / (4.0 * two_pi)
LANES = 128
RING = 8
CABLES = 2
DEFER = 4
RELAY = 2
FAR_AT = 1
FIRST = 20
LIMIT = 48
f32 = jnp.float32
bf16 = jnp.bfloat16


def halves(x):
    high = x.astype(bf16)
    return high, (x - high.astype(f32)).astype(bf16)


def running_sum(rows, sublane):
    rows = list(rows)
    for k in range(1, len(rows)):
        rows[k] = rows[k] + rows[k - 1]
    before = rows[-1]
    for shift in (1, 2, 4):
        before = before + jnp.where(sublane >= shift, pltpu.roll(before, shift, 0), 0.0)
    before = jnp.where(sublane >= 1, pltpu.roll(before, 1, 0), 0.0)
    return [row + before for row in rows]


def main_kernel(
    n_tm, n_chan,
    phase, wrap, coupling, taps,
    ybuf, offset_out, edge_out, common_out,
    pbuf, wbuf, zhi, zlo, swap_in, swap_out, matrix, sums, late, ends,
    send_left, send_right, halo_left, halo_right,
    ends_in, far_send, far_in, own_row, row_in, plane_row, plane_in,
    sem_in, s_left, s_right, r_left, r_right,
    s_ends, r_ends, s_far, r_far, s_row, r_row, s_plane, r_plane,
):
    cables, times, width = phase.shape
    blocks = width // LANES
    assert times == 64
    parts = times // 16
    tm = lax.axis_index("tm")
    chan = lax.axis_index("chan")

    def load(c):
        return (
            pltpu.make_async_copy(phase.at[c], pbuf.at[c, :, pl.ds(0, width)], sem_in.at[0, c]),
            pltpu.make_async_copy(wrap.at[c], wbuf.at[c, :, pl.ds(0, width)], sem_in.at[1, c]),
        )

    for c in range(cables):
        for copy in load(c):
            copy.start()

    barrier = pltpu.get_barrier_semaphore()

    @pl.loop(1, n_chan)
    def _(d):
        pl.semaphore_signal(barrier, inc=1, device_id={"chan": chan ^ d})

    for d in range(1, n_tm):
        pl.semaphore_signal(barrier, inc=1, device_id={"tm": tm ^ d})

    lane = lax.broadcasted_iota(jnp.int32, (1, LANES), 1)

    def band(c):
        row = (jnp.where(lane == LANES // 2, 1.0, 0.0) - taps[pl.ds(c, 1), :]) * scale
        row = jnp.concatenate([row, jnp.zeros_like(row)], axis=1)
        high = row.astype(bf16).astype(f32)
        for i, part in enumerate((high, row - high)):
            spread = jnp.broadcast_to(part, (LANES, 2 * LANES))
            turned = pltpu.roll(spread, 0, 1, stride=1, stride_axis=0)
            matrix[c, i * LANES : (i + 1) * LANES, :] = turned.astype(bf16)

    @pl.loop(0, cables, step=4)
    def _(c):
        for k in range(4):
            band(c + k)

    sublane = lax.broadcasted_iota(jnp.int32, (8, LANES), 0)
    left = lax.broadcasted_iota(jnp.int32, (8, LANES), 1) < LANES // 2
    sums[...] = jnp.zeros_like(sums)
    ends[:, blocks:, :] = jnp.zeros((cables, 8, LANES), f32)

    @pl.when(chan == 0)
    def _():
        halo_left[...] = jnp.zeros_like(halo_left)

    @pl.when(chan == n_chan - 1)
    def _():
        halo_right[...] = jnp.zeros_like(halo_right)

    def to_left(c):
        return pltpu.make_async_remote_copy(
            send_left.at[c], halo_right.at[c], s_left.at[c], r_right.at[c],
            device_id={"chan": chan - 1},
        )

    def to_right(c):
        return pltpu.make_async_remote_copy(
            send_right.at[c], halo_left.at[c], s_right.at[c], r_left.at[c],
            device_id={"chan": chan + 1},
        )

    def later(d, src, dst, send, recv):
        return pltpu.make_async_remote_copy(src, dst, send, recv, device_id={"tm": tm + d})

    def ends_to(d, src, dst):
        return later(d, src, dst, s_ends.at[d - 1], r_ends.at[d - 1])

    def far_to(d):
        return later(d, far_send, far_in.at[tm], s_far.at[d - 1], r_far.at[d - 1])

    def row_to(d):
        return later(d, own_row, row_in.at[tm], s_row.at[d - 1], r_row.at[d - 1])

    def for_later(action):
        for d in range(1, n_tm):
            pl.when(tm + d < n_tm)(functools.partial(action, d))

    def from_earlier(action):
        for d in range(1, n_tm):
            pl.when(tm - d >= 0)(functools.partial(action, d))

    def put(c, at, rows):
        for i in range(parts):
            high, low = halves(jnp.concatenate(rows[2 * i : 2 * i + 2], axis=0))
            zhi[c, i, at] = high
            zlo[c, i, at] = low

    def turn(row):
        return pltpu.roll(row, LANES // 2, 1)

    def spread(c, b, previous, ready):
        col = slice(b * LANES, (b + 1) * LANES)
        for i in range(8):
            at = slice(8 * i, 8 * i + 8)
            if b < blocks:
                step = pbuf[c, at, col]
                if not ready:
                    step = step + two_pi * wbuf[c, at, col].astype(f32)
                turned = turn(step)
            else:
                turned = jnp.zeros((8, LANES), f32)
            swap_in[b][pl.ds(25 * i, 8, stride=3), :] = jnp.where(left, previous[i], turned)
            previous[i] = turned

    def scan(b):
        rows = [swap_in[b][pl.ds(3 * k, 8, stride=25), :] for k in range(8)]
        for k, row in enumerate(running_sum(rows, sublane)):
            swap_out[b][pl.ds(3 * k, 8, stride=25), :] = row

    def scanned(b):
        return [swap_out[b][pl.ds(25 * i, 8, stride=3), :] for i in range(8)]

    def keep_edge(c, b, rows):
        for edge, buffer in ((0, send_left), (blocks, send_right)):
            if b == edge:
                for i, row in enumerate(rows):
                    buffer[c, 8 * i : 8 * i + 8, :] = row

    def collect(c, b, total):
        rows = scanned(b)
        if total is not None:
            for i, row in enumerate(rows):
                total[i] = total[i] + row
        ends[c, b : b + 1, :] = rows[-1][7:8, :]
        if total is not None:
            keep_edge(c, b, rows)
        put(c, b, rows)

    def accumulate(c, ready=False):
        previous = [jnp.zeros((8, LANES), f32)] * 8
        total = None if ready else [sums[8 * i : 8 * i + 8, :] for i in range(8)]
        for b in range(blocks + 1):
            spread(c, b, previous, ready)
            scan(b)
            collect(c, b, total)
        if not ready:
            for i, row in enumerate(total):
                sums[8 * i : 8 * i + 8, :] = row

    def edges(c):
        spread(c, 0, [jnp.zeros((8, LANES), f32)] * 8, True)
        spread(c, blocks, [turn(pbuf[c, 8 * i : 8 * i + 8, width - LANES : width]) for i in range(8)], True)
        for b in (0, blocks):
            scan(b)
            keep_edge(c, b, scanned(b))

    def increments(c):
        total = [late[8 * i : 8 * i + 8, :] for i in range(8)]
        for w in range(blocks):
            col = slice(w * LANES, (w + 1) * LANES)
            for i in range(8):
                at = slice(8 * i, 8 * i + 8)
                step = pbuf[c, at, col] + two_pi * wbuf[c, at, col].astype(f32)
                pbuf[c, at, col] = step
                total[i] = total[i] + step
        for i, row in enumerate(total):
            late[8 * i : 8 * i + 8, :] = row

    def arrived(c):
        for copy in load(c):
            copy.wait()

    def send_edges(c):
        @pl.when(chan > 0)
        def _():
            to_left(c).start()

        @pl.when(chan < n_chan - 1)
        def _():
            to_right(c).start()

    def send_ends(c):
        for_later(lambda d: ends_to(d, ends.at[c], ends_in.at[tm, c]).start())

    @pl.loop(0, cables - DEFER)
    def _(c):
        arrived(c)
        accumulate(c)

    pl.semaphore_wait(barrier, n_chan - 1 + n_tm - 1)

    pl.loop(0, cables - DEFER)(send_edges)

    late[...] = jnp.zeros_like(late)

    @pl.loop(cables - DEFER, cables)
    def _(c):
        arrived(c)
        increments(c)
        edges(c)
        send_edges(c)

    for i in range(8):
        swap_in[0][pl.ds(25 * i, 8, stride=3), :] = late[8 * i : 8 * i + 8, :]
    scan(0)
    for i in range(8):
        sums[8 * i : 8 * i + 8, :] += swap_out[0][pl.ds(25 * i, 8, stride=3), :]

    both = jnp.concatenate([sums[...], jnp.zeros_like(sums)], axis=0)
    own_row[...] = jnp.sum(both.T, axis=0, keepdims=True)
    for_later(lambda d: row_to(d).start())
    pl.loop(0, cables - DEFER)(send_ends)

    def to_plane(d):
        return pltpu.make_async_remote_copy(
            plane_row, plane_in.at[chan], s_plane, r_plane, device_id={"chan": chan ^ d}
        )

    def relay_row():
        from_earlier(lambda d: row_to(d).wait_recv())
        row = own_row[...]
        for source in range(n_tm - 1):
            last = row_in[source][:, times - 1 : times]
            row = row + jnp.where(source < tm, last, 0.0)
        plane_row[...] = row
        plane_in[chan] = row
        for d in range(1, n_chan):
            to_plane(d ^ FIRST if d != FIRST else FIRST).start()

    @pl.loop(cables - DEFER, cables)
    def _(c):
        pl.when(c == cables - DEFER + RELAY)(relay_row)
        accumulate(c, ready=True)
        send_ends(c)

    def window(z, c, w):
        return jnp.concatenate(
            [jnp.concatenate([z[c, i, w], z[c, i, w + 1]], axis=1) for i in range(parts)],
            axis=0,
        )

    def push(c, register):
        for mxu in range(2):
            pltpu.matmul_push_rhs(matrix[c], register, mxu, transpose=True)

    def joined(acc):
        pair = pltpu.matmul_pop(acc)
        return pair[:, :LANES] + pair[:, LANES:]

    def filtered(first, acc):
        order = [*range(1, blocks - 1), 0, blocks - 1]
        work = [(first + k, w, n, k) for k in range(CABLES) for n, w in enumerate(order)]

        def finish(m):
            c, w, _, _ = work[m]
            ybuf[c, :, w * LANES : (w + 1) * LANES] = joined(acc[m % RING])

        push(first, 0)
        for m, (c, w, n, k) in enumerate(work):
            if m >= RING:
                finish(m - RING)
            fresh = k % 2 if n < 2 else None
            pltpu.matmul_acc_lhs(acc[m % RING], window(zhi, c, w), fresh)
            pltpu.matmul_acc_lhs(acc[m % RING], window(zlo, c, w))
            if n == 2 and k + 1 < CABLES:
                push(c + 1, (k + 1) % 2)
        for m in range(len(work) - RING, len(work)):
            finish(m)

    def all_plane():
        others = plane_in.at[pl.ds(0, n_chan - 1)]
        return pltpu.make_async_remote_copy(
            others, others, s_plane, r_plane, device_id={"chan": chan ^ 1}
        )

    def halos(c):
        @pl.when(chan > 0)
        def _():
            to_right(c).wait_recv()

        @pl.when(chan < n_chan - 1)
        def _():
            to_left(c).wait_recv()

    def relay_far():
        pl.loop(FAR_AT * CABLES, cables)(halos)
        inner = left[:1]
        for c in range(cables):
            last = slice(times - 1, times)
            far_send[c : c + 1, :] = jnp.where(inner, halo_left[c, last, :], 0.0)
            far_send[cables + c : cables + c + 1, :] = jnp.where(inner, 0.0, halo_right[c, last, :])
        for_later(lambda d: far_to(d).start())

    @pl.loop(0, cables // CABLES)
    def _(k):
        pl.when(k == FAR_AT)(relay_far)

        @pl.when(k < FAR_AT)
        def _():
            for j in range(CABLES):
                halos(k * CABLES + j)

        def tile(buffer, c, i):
            return buffer[c, 8 * i : 8 * i + 8, :]

        for j in range(CABLES):
            c = k * CABLES + j
            for at, low, high in ((0, halo_left, send_left), (blocks, send_right, halo_right)):
                put(c, at, [jnp.where(left, tile(low, c, i), tile(high, c, i)) for i in range(8)])
        pl.run_scoped(
            lambda *acc: filtered(k * CABLES, acc),
            *[pltpu.ACC(n % 2)((times, 2 * LANES), f32) for n in range(RING)],
        )

    from_earlier(lambda d: ends_to(d, ends, ends_in.at[tm]).wait_recv())
    from_earlier(lambda d: far_to(d).wait_recv())
    far = jnp.zeros_like(far_send)
    for source in range(n_tm - 1):
        far = far + jnp.where(source < tm, far_in[source], 0.0)

    padded = blocks + 8
    row_of = lax.broadcasted_iota(jnp.int32, (padded, LANES), 0)
    position = row_of[:blocks]
    ones = jnp.ones((16, LANES), f32)
    which = lax.broadcasted_iota(jnp.int32, (16, LANES), 0)
    half = lax.broadcasted_iota(jnp.int32, (16, LANES), 1) < LANES // 2
    one_rows = jnp.concatenate(
        [
            jnp.where((which == 1) & half, 0.0, ones).astype(bf16),
            jnp.where((which == 2) & ~half, 0.0, ones).astype(bf16),
        ],
        axis=1,
    )

    def constants(*accs):
        for c in range(cables):
            mxu, small, constant = c % 2, accs[2 * c], accs[2 * c + 1]
            here = jnp.zeros((padded, LANES), f32)
            for source in range(n_tm - 1):
                here = here + jnp.where(source < tm, ends_in[source, c], 0.0)
            here = here + jnp.where(row_of == 0, far[c : c + 1, :], 0.0)
            here = here + jnp.where(row_of == blocks, far[cables + c : cables + c + 1, :], 0.0)
            after = pltpu.roll(here, padded - 1, 0)[:blocks]
            pltpu.matmul_push_rhs(matrix[c], 0, mxu, transpose=True)
            for i, pair in enumerate(zip(halves(here[:blocks]), halves(after))):
                pltpu.matmul_acc_lhs(small, jnp.concatenate(pair, axis=1), None if i else 0)
            pltpu.matmul_acc_lhs(constant, one_rows)
        for c in range(cables):
            offset_out[c] = joined(accs[2 * c])
            flat = joined(accs[2 * c + 1]) * coupling[c]
            edge = jnp.broadcast_to(flat[0:1, :], (blocks, LANES))
            edge = jnp.where((position == 0) & (chan == 0), flat[1:2, :], edge)
            edge = jnp.where((position == blocks - 1) & (chan == n_chan - 1), flat[2:3, :], edge)
            edge_out[c] = edge

    pl.run_scoped(
        constants,
        *[
            pltpu.ACC(c % 2)((size, 2 * LANES), f32)
            for c in range(cables)
            for size in (blocks, 16)
        ],
    )

    for_later(lambda d: row_to(d).wait_send())
    for_later(lambda d: far_to(d).wait_send())
    for_later(lambda d: ends_to(d, ends, ends_in.at[tm]).wait_send())

    @pl.loop(0, cables)
    def _(c):
        @pl.when(chan > 0)
        def _():
            to_left(c).wait_send()

        @pl.when(chan < n_chan - 1)
        def _():
            to_right(c).wait_send()

    all_plane().wait_send()
    all_plane().wait_recv()
    row = jnp.sum(plane_in[...], axis=0) * (1.0 / (cables * blocks * LANES * n_chan))
    common_out[...] = jnp.broadcast_to(row, (LANES, LANES)).T[:times]


def final_kernel(y, offset, edge, common, out, buffer, sem):
    cables, _, width = y.shape

    def copy(c):
        return pltpu.make_async_copy(buffer.at[c], out.at[c], sem.at[c])

    @pl.loop(0, cables)
    def _(c):
        mode = common[...]
        for j in range(width // LANES):
            col = slice(j * LANES, (j + 1) * LANES)
            shift = offset[c, j : j + 1, :] - mode * edge[c, j : j + 1, :]
            buffer[c, :, col] = y[c, :, col] + shift
        copy(c).start()

    @pl.loop(0, cables)
    def _(c):
        copy(c).wait()


def shards(phase_step, wrap_count, coupling, filter_taps):
    cables, times, width = phase_step.shape
    blocks = width // LANES
    n_tm, n_chan = lax.axis_size("tm"), lax.axis_size("chan")
    vmem, dma = pltpu.VMEM, pltpu.SemaphoreType.DMA
    full = (cables, times, width)
    wide = (cables, times, width + LANES)
    edge = (cables + 1, times, LANES)
    z = (cables, times // 16, blocks + 1, 16, LANES)
    small = vmem((cables, blocks, LANES), f32)
    leveled = pl.pallas_call(
        functools.partial(main_kernel, n_tm, n_chan),
        out_shape=(
            vmem(full, f32),
            small,
            small,
            vmem((times, LANES), f32),
        ),
        in_specs=[
            pl.BlockSpec(memory_space=pl.ANY),
            pl.BlockSpec(memory_space=pl.ANY),
            pl.BlockSpec(memory_space=pltpu.SMEM),
            pl.BlockSpec(memory_space=vmem),
        ],
        out_specs=(
            pl.BlockSpec(memory_space=vmem),
            pl.BlockSpec(memory_space=vmem),
            pl.BlockSpec(memory_space=vmem),
            pl.BlockSpec(memory_space=vmem),
        ),
        scratch_shapes=[
            vmem(wide, f32), vmem(wide, jnp.int32), vmem(z, bf16), vmem(z, bf16),
            [vmem((200, LANES), f32)] * (blocks + 1), [vmem((200, LANES), f32)] * (blocks + 1),
            vmem((cables, 2 * LANES, 2 * LANES), bf16),
            vmem((times, LANES), f32), vmem((times, LANES), f32), vmem((cables, blocks + 8, LANES), f32),
            vmem(edge, f32), vmem(edge, f32),
            vmem((cables, times, LANES), f32), vmem((cables, times, LANES), f32),
            vmem((n_tm, cables, blocks + 8, LANES), f32),
            vmem((2 * cables, LANES), f32), vmem((n_tm, 2 * cables, LANES), f32),
            vmem((1, LANES), f32), vmem((n_tm, 1, LANES), f32),
            vmem((1, LANES), f32), vmem((n_chan, 1, LANES), f32),
            dma((2, cables)), dma((cables,)), dma((cables,)), dma((cables,)), dma((cables,)),
            dma((n_tm - 1,)), dma((n_tm - 1,)),
            dma((n_tm - 1,)), dma((n_tm - 1,)),
            dma((n_tm - 1,)), dma((n_tm - 1,)),
            dma, dma,
        ],
        compiler_params=pltpu.CompilerParams(
            collective_id=0, has_side_effects=True, vmem_limit_bytes=LIMIT << 20
        ),
        name="level",
    )(phase_step, wrap_count, coupling, filter_taps)
    return pl.pallas_call(
        final_kernel,
        out_shape=jax.ShapeDtypeStruct(full, f32),
        in_specs=[pl.BlockSpec(memory_space=vmem)] * 4,
        out_specs=pl.BlockSpec(memory_space=pl.ANY),
        scratch_shapes=[vmem(full, f32), dma((cables,))],
        compiler_params=pltpu.CompilerParams(vmem_limit_bytes=16 << 20),
        name="finish",
    )(*[pltpu.with_memory_space_constraint(x, vmem) for x in leveled])


def solution(mesh):
    placed = (P(None, "tm", "chan"), P(None, "tm", "chan"), P(), P())
    return jax.shard_map(
        shards, mesh=mesh, in_specs=placed, out_specs=P(None, "tm", "chan"), check_vma=False
    )
```

```python
import functools
import math

import jax
import jax.numpy as jnp
from jax import lax
from jax.experimental import pallas as pl
from jax.experimental.pallas import tpu as pltpu
from jax.sharding import PartitionSpec as P

two_pi = 2.0 * math.pi
scale = 1.0 / (4.0 * two_pi)
LANES = 128
RING = 8
CABLES = 2
DEFER = 4
EARLY = 2
RELAY = 1
FIRST = 20
LIMIT = 48
f32 = jnp.float32
bf16 = jnp.bfloat16


def halves(x):
    high = x.astype(bf16)
    return high, (x - high.astype(f32)).astype(bf16)


def running_sum(rows, sublane):
    rows = list(rows)
    for k in range(1, len(rows)):
        rows[k] = rows[k] + rows[k - 1]
    before = rows[-1]
    for shift in (1, 2, 4):
        before = before + jnp.where(sublane >= shift, pltpu.roll(before, shift, 0), 0.0)
    before = jnp.where(sublane >= 1, pltpu.roll(before, 1, 0), 0.0)
    return [row + before for row in rows]


def main_kernel(
    n_tm, n_chan,
    phase, wrap, coupling, taps,
    ybuf, offset_out, edge_out, common_out,
    pbuf, wbuf, zhi, zlo, swap_in, swap_out, matrix, sums, late, ends,
    send_left, send_right, packed_left, packed_right, halo_left, halo_right,
    ends_in, far_send, far_in, own_row, row_in, plane_row, plane_in,
    sem_in, s_left, s_right, r_left, r_right,
    s_ends, r_ends, s_far, r_far, s_row, r_row, s_plane, r_plane,
):
    cables, times, width = phase.shape
    blocks = width // LANES
    assert times == 64
    parts = times // 16
    tm = lax.axis_index("tm")
    chan = lax.axis_index("chan")

    def load(c):
        return (
            pltpu.make_async_copy(phase.at[c], pbuf.at[c, :, pl.ds(0, width)], sem_in.at[0, c]),
            pltpu.make_async_copy(wrap.at[c], wbuf.at[c, :, pl.ds(0, width)], sem_in.at[1, c]),
        )

    for c in range(cables):
        for copy in load(c):
            copy.start()

    barrier = pltpu.get_barrier_semaphore()

    @pl.loop(1, n_chan)
    def _(d):
        pl.semaphore_signal(barrier, inc=1, device_id={"chan": chan ^ d})

    for d in range(1, n_tm):
        pl.semaphore_signal(barrier, inc=1, device_id={"tm": tm ^ d})

    lane = lax.broadcasted_iota(jnp.int32, (1, LANES), 1)

    def band(c):
        row = (jnp.where(lane == LANES // 2, 1.0, 0.0) - taps[pl.ds(c, 1), :]) * scale
        row = jnp.concatenate([row, jnp.zeros_like(row)], axis=1)
        high = row.astype(bf16).astype(f32)
        for i, part in enumerate((high, row - high)):
            spread = jnp.broadcast_to(part, (LANES, 2 * LANES))
            turned = pltpu.roll(spread, 0, 1, stride=1, stride_axis=0)
            matrix[c, i * LANES : (i + 1) * LANES, :] = turned.astype(bf16)

    @pl.loop(0, cables, step=4)
    def _(c):
        for k in range(4):
            band(c + k)

    sublane = lax.broadcasted_iota(jnp.int32, (8, LANES), 0)
    left = lax.broadcasted_iota(jnp.int32, (8, LANES), 1) < LANES // 2
    sums[...] = jnp.zeros_like(sums)

    @pl.when(chan == 0)
    def _():
        halo_left[...] = jnp.zeros_like(halo_left)

    @pl.when(chan == n_chan - 1)
    def _():
        halo_right[...] = jnp.zeros_like(halo_right)

    def to_left(c):
        return pltpu.make_async_remote_copy(
            packed_left.at[c], halo_right.at[c], s_left.at[c], r_right.at[c],
            device_id={"chan": chan - 1},
        )

    def to_right(c):
        return pltpu.make_async_remote_copy(
            packed_right.at[c], halo_left.at[c], s_right.at[c], r_left.at[c],
            device_id={"chan": chan + 1},
        )

    def later(d, src, dst, send, recv):
        return pltpu.make_async_remote_copy(src, dst, send, recv, device_id={"tm": tm + d})

    def ends_to(d, src, dst):
        return later(d, src, dst, s_ends.at[d - 1], r_ends.at[d - 1])

    def far_to(d):
        return later(d, far_send, far_in.at[tm], s_far.at[d - 1], r_far.at[d - 1])

    def row_to(d):
        return later(d, own_row, row_in.at[tm], s_row.at[d - 1], r_row.at[d - 1])

    def for_later(action):
        for d in range(1, n_tm):
            pl.when(tm + d < n_tm)(functools.partial(action, d))

    def from_earlier(action):
        for d in range(1, n_tm):
            pl.when(tm - d >= 0)(functools.partial(action, d))

    def put(c, at, rows):
        for i in range(parts):
            high, low = halves(jnp.concatenate(rows[2 * i : 2 * i + 2], axis=0))
            zhi[c, i, at] = high
            zlo[c, i, at] = low

    def turn(row):
        return pltpu.roll(row, LANES // 2, 1)

    def spread(c, b, previous, ready):
        col = slice(b * LANES, (b + 1) * LANES)
        for i in range(8):
            at = slice(8 * i, 8 * i + 8)
            if b < blocks:
                step = pbuf[c, at, col]
                if not ready:
                    step = step + two_pi * wbuf[c, at, col].astype(f32)
                turned = turn(step)
            else:
                turned = jnp.zeros((8, LANES), f32)
            swap_in[b][pl.ds(25 * i, 8, stride=3), :] = jnp.where(left, previous[i], turned)
            previous[i] = turned

    def scan(b):
        rows = [swap_in[b][pl.ds(3 * k, 8, stride=25), :] for k in range(8)]
        for k, row in enumerate(running_sum(rows, sublane)):
            swap_out[b][pl.ds(3 * k, 8, stride=25), :] = row

    def scanned(b):
        return [swap_out[b][pl.ds(25 * i, 8, stride=3), :] for i in range(8)]

    def keep_edge(c, b, rows):
        for edge, buffer in ((0, send_left), (blocks, send_right)):
            if b == edge:
                for i, row in enumerate(rows):
                    buffer[c, 8 * i : 8 * i + 8, :] = row
                for i in range(4):
                    at = slice(8 * i, 8 * i + 8)
                    late_rows = turn(rows[i + 4])
                    if edge:
                        packed_right[c, at, :] = jnp.where(left, rows[i], late_rows)
                    else:
                        packed_left[c, at, :] = jnp.where(left, late_rows, rows[i])

    def collect(c, b, total):
        rows = scanned(b)
        if total is not None:
            for i, row in enumerate(rows):
                total[i] = total[i] + row
        last = rows[-1][7:8, :]
        if b == blocks:
            last = jnp.where(left[:1], last, ends[c, 0:1, :])
        ends[c, b % blocks : b % blocks + 1, :] = last
        if total is not None:
            keep_edge(c, b, rows)
        put(c, b, rows)

    def accumulate(c, ready=False):
        previous = [jnp.zeros((8, LANES), f32)] * 8
        total = None if ready else [sums[8 * i : 8 * i + 8, :] for i in range(8)]
        for b in range(blocks + 1):
            spread(c, b, previous, ready)
            scan(b)
            collect(c, b, total)
        if not ready:
            for i, row in enumerate(total):
                sums[8 * i : 8 * i + 8, :] = row

    def edges(c):
        spread(c, 0, [jnp.zeros((8, LANES), f32)] * 8, True)
        spread(c, blocks, [turn(pbuf[c, 8 * i : 8 * i + 8, width - LANES : width]) for i in range(8)], True)
        for b in (0, blocks):
            scan(b)
            keep_edge(c, b, scanned(b))

    def increments(c):
        total = [late[8 * i : 8 * i + 8, :] for i in range(8)]
        for w in range(blocks):
            col = slice(w * LANES, (w + 1) * LANES)
            for i in range(8):
                at = slice(8 * i, 8 * i + 8)
                step = pbuf[c, at, col] + two_pi * wbuf[c, at, col].astype(f32)
                pbuf[c, at, col] = step
                total[i] = total[i] + step
        for i, row in enumerate(total):
            late[8 * i : 8 * i + 8, :] = row

    def arrived(c):
        for copy in load(c):
            copy.wait()

    def send_edges(c):
        @pl.when(chan > 0)
        def _():
            to_left(c).start()

        @pl.when(chan < n_chan - 1)
        def _():
            to_right(c).start()

    def send_ends(c):
        for_later(lambda d: ends_to(d, ends.at[c], ends_in.at[tm, c]).start())

    @pl.loop(0, cables - DEFER)
    def _(c):
        arrived(c)
        accumulate(c)

    pl.semaphore_wait(barrier, n_chan - 1 + n_tm - 1)

    pl.loop(0, cables - DEFER)(send_edges)
    pl.loop(0, EARLY)(send_ends)

    late[...] = jnp.zeros_like(late)

    @pl.loop(cables - DEFER, cables)
    def _(c):
        arrived(c)
        increments(c)
        edges(c)
        send_edges(c)

    for i in range(8):
        swap_in[0][pl.ds(25 * i, 8, stride=3), :] = late[8 * i : 8 * i + 8, :]
    scan(0)
    for i in range(8):
        sums[8 * i : 8 * i + 8, :] += swap_out[0][pl.ds(25 * i, 8, stride=3), :]

    both = jnp.concatenate([sums[...], jnp.zeros_like(sums)], axis=0)
    own_row[...] = jnp.sum(both.T, axis=0, keepdims=True)
    for_later(lambda d: row_to(d).start())
    pl.loop(EARLY, cables - DEFER)(send_ends)

    def to_plane(d):
        return pltpu.make_async_remote_copy(
            plane_row, plane_in.at[chan], s_plane, r_plane, device_id={"chan": chan ^ d}
        )

    def relay_row():
        from_earlier(lambda d: row_to(d).wait_recv())
        row = own_row[...]
        for source in range(n_tm - 1):
            last = row_in[source][:, times - 1 : times]
            row = row + jnp.where(source < tm, last, 0.0)
        plane_row[...] = row
        plane_in[chan] = row
        for d in range(1, n_chan):
            to_plane(d ^ FIRST if d != FIRST else FIRST).start()

    def window(z, c, w):
        return jnp.concatenate(
            [jnp.concatenate([z[c, i, w], z[c, i, w + 1]], axis=1) for i in range(parts)],
            axis=0,
        )

    def push(c, register):
        for mxu in range(2):
            pltpu.matmul_push_rhs(matrix[c], register, mxu, transpose=True)

    def joined(acc):
        pair = pltpu.matmul_pop(acc)
        return pair[:, :LANES] + pair[:, LANES:]

    def filtered(first, acc, outer):
        order = [*range(1, blocks - 1)] + [0, blocks - 1] * outer
        work = [(first + k, w, n, k) for k in range(CABLES) for n, w in enumerate(order)]

        def finish(m):
            c, w, _, _ = work[m]
            ybuf[c, :, w * LANES : (w + 1) * LANES] = joined(acc[m % RING])

        push(first, 0)
        for m, (c, w, n, k) in enumerate(work):
            if m >= RING:
                finish(m - RING)
            fresh = k % 2 if n < 2 else None
            pltpu.matmul_acc_lhs(acc[m % RING], window(zhi, c, w), fresh)
            pltpu.matmul_acc_lhs(acc[m % RING], window(zlo, c, w))
            if n == 2 and k + 1 < CABLES:
                push(c + 1, (k + 1) % 2)
        for m in range(len(work) - RING, len(work)):
            finish(m)

    def all_plane():
        others = plane_in.at[pl.ds(0, n_chan - 1)]
        return pltpu.make_async_remote_copy(
            others, others, s_plane, r_plane, device_id={"chan": chan ^ 1}
        )

    def halos(c):
        @pl.when(chan > 0)
        def _():
            to_right(c).wait_recv()

        @pl.when(chan < n_chan - 1)
        def _():
            to_left(c).wait_recv()

    def relay_far():
        pl.loop(0, cables)(halos)
        last = slice(times // 2 - 1, times // 2)
        halo_rows = [halo[c, last, :] for halo in (halo_left, halo_right) for c in range(cables)]
        halo_rows = turn(jnp.concatenate(halo_rows, axis=0))
        from_left = lax.broadcasted_iota(jnp.int32, halo_rows.shape, 0) < cables
        low = lax.broadcasted_iota(jnp.int32, halo_rows.shape, 1) < LANES // 2
        far_send[...] = jnp.where(from_left == low, halo_rows, 0.0)
        for_later(lambda d: far_to(d).start())

    def edge_blocks(k):
        def tile(buffer, c, i):
            if buffer is send_left or buffer is send_right:
                return buffer[c, 8 * i : 8 * i + 8, :]
            packed = buffer[c, 8 * (i % 4) : 8 * (i % 4) + 8, :]
            return packed if i < 4 else turn(packed)

        for c in (k * CABLES + j for j in range(CABLES)):
            for at, low, high in ((0, halo_left, send_left), (blocks, send_right, halo_right)):
                put(c, at, [jnp.where(left, tile(low, c, i), tile(high, c, i)) for i in range(8)])

    def matmuls(body):
        pl.run_scoped(body, *[pltpu.ACC(n % 2)((times, 2 * LANES), f32) for n in range(RING)])

    @pl.loop(0, DEFER // CABLES)
    def _(k):
        pl.when(k == jnp.where(tm == 0, 0, RELAY))(relay_row)

        def body(*acc):
            filtered(k * CABLES, acc, False)
            for j in range(CABLES):
                accumulate(cables - DEFER + k * CABLES + j, ready=True)

        matmuls(body)
        for j in range(CABLES):
            send_ends(cables - DEFER + k * CABLES + j)

    relay_far()

    @pl.loop(DEFER // CABLES, cables // CABLES)
    def _(k):
        edge_blocks(k)
        matmuls(lambda *acc: filtered(k * CABLES, acc, True))

    from_earlier(lambda d: ends_to(d, ends, ends_in.at[tm]).wait_recv())
    from_earlier(lambda d: far_to(d).wait_recv())
    far = jnp.zeros_like(far_send)
    for source in range(n_tm - 1):
        far = far + jnp.where(source < tm, far_in[source], 0.0)

    position = lax.broadcasted_iota(jnp.int32, (blocks, LANES), 0)
    low_half = lax.broadcasted_iota(jnp.int32, (blocks, LANES), 1) < LANES // 2
    ones = jnp.ones((16, LANES), f32)
    which = lax.broadcasted_iota(jnp.int32, (16, LANES), 0)
    half = lax.broadcasted_iota(jnp.int32, (16, LANES), 1) < LANES // 2
    one_rows = jnp.concatenate(
        [
            jnp.where((which == 1) & half, 0.0, ones).astype(bf16),
            jnp.where((which == 2) & ~half, 0.0, ones).astype(bf16),
        ],
        axis=1,
    )

    for k in range(DEFER // CABLES):
        edge_blocks(k)

    def constants(*accs):
        outer = accs[2 * cables :]
        for c in range(cables):
            mxu, small, constant = c % 2, accs[2 * c], accs[2 * c + 1]
            own = jnp.zeros((blocks, LANES), f32)
            for source in range(n_tm - 1):
                own = own + jnp.where(source < tm, ends_in[source, c], 0.0)
            here = jnp.where((position == 0) & low_half, far[c : c + 1, :], own)
            after = jnp.where(
                (position == blocks - 1) & ~low_half,
                far[cables + c : cables + c + 1, :],
                pltpu.roll(own, blocks - 1, 0),
            )
            pltpu.matmul_push_rhs(matrix[c], 0, mxu, transpose=True)
            for i, pair in enumerate(zip(halves(here), halves(after))):
                pltpu.matmul_acc_lhs(small, jnp.concatenate(pair, axis=1), None if i else 0)
            pltpu.matmul_acc_lhs(constant, one_rows)
            if c < DEFER:
                for acc, w in zip(outer[2 * c :], (0, blocks - 1)):
                    pltpu.matmul_acc_lhs(acc, window(zhi, c, w))
                    pltpu.matmul_acc_lhs(acc, window(zlo, c, w))
        for c in range(cables):
            offset_out[c] = joined(accs[2 * c])
            if c < DEFER:
                for acc, w in zip(outer[2 * c :], (0, blocks - 1)):
                    ybuf[c, :, w * LANES : (w + 1) * LANES] = joined(acc)
            flat = joined(accs[2 * c + 1]) * coupling[c]
            edge = jnp.broadcast_to(flat[0:1, :], (blocks, LANES))
            edge = jnp.where((position == 0) & (chan == 0), flat[1:2, :], edge)
            edge = jnp.where((position == blocks - 1) & (chan == n_chan - 1), flat[2:3, :], edge)
            edge_out[c] = edge

    pl.run_scoped(
        constants,
        *[
            pltpu.ACC(c % 2)((size, 2 * LANES), f32)
            for c in range(cables)
            for size in (blocks, 16)
        ],
        *[pltpu.ACC(c % 2)((times, 2 * LANES), f32) for c in range(DEFER) for _ in range(2)],
    )

    for_later(lambda d: row_to(d).wait_send())
    for_later(lambda d: far_to(d).wait_send())
    for_later(lambda d: ends_to(d, ends, ends_in.at[tm]).wait_send())

    @pl.loop(0, cables)
    def _(c):
        @pl.when(chan > 0)
        def _():
            to_left(c).wait_send()

        @pl.when(chan < n_chan - 1)
        def _():
            to_right(c).wait_send()

    all_plane().wait_send()
    all_plane().wait_recv()
    row = jnp.sum(plane_in[...], axis=0) * (1.0 / (cables * blocks * LANES * n_chan))
    common_out[...] = jnp.broadcast_to(row, (LANES, LANES)).T[:times]


def final_kernel(y, offset, edge, common, out, buffer, sem):
    cables, _, width = y.shape

    def copy(c):
        return pltpu.make_async_copy(buffer.at[c], out.at[c], sem.at[c])

    @pl.loop(0, cables)
    def _(c):
        mode = common[...]
        for j in range(width // LANES):
            col = slice(j * LANES, (j + 1) * LANES)
            shift = offset[c, j : j + 1, :] - mode * edge[c, j : j + 1, :]
            buffer[c, :, col] = y[c, :, col] + shift
        copy(c).start()

    @pl.loop(0, cables)
    def _(c):
        copy(c).wait()


def shards(phase_step, wrap_count, coupling, filter_taps):
    cables, times, width = phase_step.shape
    blocks = width // LANES
    n_tm, n_chan = lax.axis_size("tm"), lax.axis_size("chan")
    vmem, dma = pltpu.VMEM, pltpu.SemaphoreType.DMA
    full = (cables, times, width)
    wide = (cables, times, width + LANES)
    edge = (cables + 1, times, LANES)
    z = (cables, times // 16, blocks + 1, 16, LANES)
    small = vmem((cables, blocks, LANES), f32)
    leveled = pl.pallas_call(
        functools.partial(main_kernel, n_tm, n_chan),
        out_shape=(
            vmem(full, f32),
            small,
            small,
            vmem((times, LANES), f32),
        ),
        in_specs=[
            pl.BlockSpec(memory_space=pl.ANY),
            pl.BlockSpec(memory_space=pl.ANY),
            pl.BlockSpec(memory_space=pltpu.SMEM),
            pl.BlockSpec(memory_space=vmem),
        ],
        out_specs=(
            pl.BlockSpec(memory_space=vmem),
            pl.BlockSpec(memory_space=vmem),
            pl.BlockSpec(memory_space=vmem),
            pl.BlockSpec(memory_space=vmem),
        ),
        scratch_shapes=[
            vmem(wide, f32), vmem(wide, jnp.int32), vmem(z, bf16), vmem(z, bf16),
            [vmem((200, LANES), f32)] * (blocks + 1), [vmem((200, LANES), f32)] * (blocks + 1),
            vmem((cables, 2 * LANES, 2 * LANES), bf16),
            vmem((times, LANES), f32), vmem((times, LANES), f32), vmem((cables, blocks, LANES), f32),
            vmem(edge, f32), vmem(edge, f32),
            *[vmem((cables, times // 2, LANES), f32)] * 4,
            vmem((n_tm, cables, blocks, LANES), f32),
            vmem((2 * cables, LANES), f32), vmem((n_tm, 2 * cables, LANES), f32),
            vmem((1, LANES), f32), vmem((n_tm, 1, LANES), f32),
            vmem((1, LANES), f32), vmem((n_chan, 1, LANES), f32),
            dma((2, cables)), dma((cables,)), dma((cables,)), dma((cables,)), dma((cables,)),
            dma((n_tm - 1,)), dma((n_tm - 1,)),
            dma((n_tm - 1,)), dma((n_tm - 1,)),
            dma((n_tm - 1,)), dma((n_tm - 1,)),
            dma, dma,
        ],
        compiler_params=pltpu.CompilerParams(
            collective_id=0, has_side_effects=True, vmem_limit_bytes=LIMIT << 20
        ),
        name="level",
    )(phase_step, wrap_count, coupling, filter_taps)
    return pl.pallas_call(
        final_kernel,
        out_shape=jax.ShapeDtypeStruct(full, f32),
        in_specs=[pl.BlockSpec(memory_space=vmem)] * 4,
        out_specs=pl.BlockSpec(memory_space=pl.ANY),
        scratch_shapes=[vmem(full, f32), dma((cables,))],
        compiler_params=pltpu.CompilerParams(vmem_limit_bytes=16 << 20),
        name="finish",
    )(*[pltpu.with_memory_space_constraint(x, vmem) for x in leveled])


def solution(mesh):
    placed = (P(None, "tm", "chan"), P(None, "tm", "chan"), P(), P())
    return jax.shard_map(
        shards, mesh=mesh, in_specs=placed, out_specs=P(None, "tm", "chan"), check_vma=False
    )
```

```python
import functools
import math

import jax
import jax.numpy as jnp
from jax import lax
from jax.experimental import pallas as pl
from jax.experimental.pallas import tpu as pltpu
from jax.sharding import PartitionSpec as P

two_pi = 2.0 * math.pi
scale = 1.0 / (4.0 * two_pi)
LANES = 128
RING = 8
CABLES = 2
DEFER = 4
EARLY = 2
RELAY = 1
LIMIT = 48
f32 = jnp.float32
bf16 = jnp.bfloat16


def halves(x):
    high = x.astype(bf16)
    return high, (x - high.astype(f32)).astype(bf16)


def running_sum(rows, sublane):
    rows = list(rows)
    for k in range(1, len(rows)):
        rows[k] = rows[k] + rows[k - 1]
    before = rows[-1]
    for shift in (1, 2, 4):
        before = before + jnp.where(sublane >= shift, pltpu.roll(before, shift, 0), 0.0)
    before = jnp.where(sublane >= 1, pltpu.roll(before, 1, 0), 0.0)
    return [row + before for row in rows]


def main_kernel(
    n_tm, n_chan,
    phase, wrap, coupling, taps,
    ybuf, offset_out, edge_out, common_out,
    pbuf, wbuf, zhi, zlo, swap_in, swap_out, matrix, sums, late, ends,
    send_left, send_right, packed_left, packed_right, halo_left, halo_right,
    ends_in, far_send, far_in, own_row, row_in, plane_row, plane_in,
    sem_in, s_left, s_right, r_left, r_right,
    s_ends, r_ends, s_far, r_far, s_row, r_row, s_plane, r_plane,
):
    cables, times, width = phase.shape
    blocks = width // LANES
    assert times == 64
    parts = times // 16
    tm = lax.axis_index("tm")
    chan = lax.axis_index("chan")

    def load(c):
        return (
            pltpu.make_async_copy(phase.at[c], pbuf.at[c, :, pl.ds(0, width)], sem_in.at[0, c]),
            pltpu.make_async_copy(wrap.at[c], wbuf.at[c, :, pl.ds(0, width)], sem_in.at[1, c]),
        )

    for c in range(cables):
        for copy in load(c):
            copy.start()

    barrier = pltpu.get_barrier_semaphore()

    @pl.loop(1, n_chan)
    def _(d):
        pl.semaphore_signal(barrier, inc=1, device_id={"chan": chan ^ d})

    for d in range(1, n_tm):
        pl.semaphore_signal(barrier, inc=1, device_id={"tm": tm ^ d})

    lane = lax.broadcasted_iota(jnp.int32, (1, LANES), 1)

    def band(c):
        row = (jnp.where(lane == LANES // 2, 1.0, 0.0) - taps[pl.ds(c, 1), :]) * scale
        row = jnp.concatenate([row, jnp.zeros_like(row)], axis=1)
        high = row.astype(bf16).astype(f32)
        for i, part in enumerate((high, row - high)):
            spread = jnp.broadcast_to(part, (LANES, 2 * LANES))
            turned = pltpu.roll(spread, 0, 1, stride=1, stride_axis=0)
            matrix[c, i * LANES : (i + 1) * LANES, :] = turned.astype(bf16)

    @pl.loop(0, cables, step=4)
    def _(c):
        for k in range(4):
            band(c + k)

    sublane = lax.broadcasted_iota(jnp.int32, (8, LANES), 0)
    left = lax.broadcasted_iota(jnp.int32, (8, LANES), 1) < LANES // 2
    sums[...] = jnp.zeros_like(sums)

    @pl.when(chan == 0)
    def _():
        halo_left[...] = jnp.zeros_like(halo_left)

    @pl.when(chan == n_chan - 1)
    def _():
        halo_right[...] = jnp.zeros_like(halo_right)

    def to_left(c):
        return pltpu.make_async_remote_copy(
            packed_left.at[c], halo_right.at[c], s_left.at[c], r_right.at[c],
            device_id={"chan": chan - 1},
        )

    def to_right(c):
        return pltpu.make_async_remote_copy(
            packed_right.at[c], halo_left.at[c], s_right.at[c], r_left.at[c],
            device_id={"chan": chan + 1},
        )

    def later(d, src, dst, send, recv):
        return pltpu.make_async_remote_copy(src, dst, send, recv, device_id={"tm": tm + d})

    def ends_to(d, src, dst):
        return later(d, src, dst, s_ends.at[d - 1], r_ends.at[d - 1])

    def far_to(d):
        return later(d, far_send, far_in.at[tm], s_far.at[d - 1], r_far.at[d - 1])

    def row_to(d):
        return later(d, own_row, row_in.at[tm], s_row.at[d - 1], r_row.at[d - 1])

    def for_later(action):
        for d in range(1, n_tm):
            pl.when(tm + d < n_tm)(functools.partial(action, d))

    def from_earlier(action):
        for d in range(1, n_tm):
            pl.when(tm - d >= 0)(functools.partial(action, d))

    def put(c, at, rows):
        for i in range(parts):
            high, low = halves(jnp.concatenate(rows[2 * i : 2 * i + 2], axis=0))
            zhi[c, i, at] = high
            zlo[c, i, at] = low

    def turn(row):
        return pltpu.roll(row, LANES // 2, 1)

    def spread(c, b, previous, ready):
        col = slice(b * LANES, (b + 1) * LANES)
        for i in range(8):
            at = slice(8 * i, 8 * i + 8)
            if b < blocks:
                step = pbuf[c, at, col]
                if not ready:
                    step = step + two_pi * wbuf[c, at, col].astype(f32)
                turned = turn(step)
            else:
                turned = jnp.zeros((8, LANES), f32)
            swap_in[b][pl.ds(25 * i, 8, stride=3), :] = jnp.where(left, previous[i], turned)
            previous[i] = turned

    def scan(b):
        rows = [swap_in[b][pl.ds(3 * k, 8, stride=25), :] for k in range(8)]
        for k, row in enumerate(running_sum(rows, sublane)):
            swap_out[b][pl.ds(3 * k, 8, stride=25), :] = row

    def scanned(b):
        return [swap_out[b][pl.ds(25 * i, 8, stride=3), :] for i in range(8)]

    def keep_edge(c, b, rows):
        for edge, buffer in ((0, send_left), (blocks, send_right)):
            if b == edge:
                for i, row in enumerate(rows):
                    buffer[c, 8 * i : 8 * i + 8, :] = row
                for i in range(4):
                    at = slice(8 * i, 8 * i + 8)
                    late_rows = turn(rows[i + 4])
                    if edge:
                        packed_right[c, at, :] = jnp.where(left, rows[i], late_rows)
                    else:
                        packed_left[c, at, :] = jnp.where(left, late_rows, rows[i])

    def collect(c, b, total):
        rows = scanned(b)
        if total is not None:
            for i, row in enumerate(rows):
                total[i] = total[i] + row
        last = rows[-1][7:8, :]
        if b == blocks:
            last = jnp.where(left[:1], last, ends[c, 0:1, :])
        ends[c, b % blocks : b % blocks + 1, :] = last
        if total is not None:
            keep_edge(c, b, rows)
        put(c, b, rows)

    def accumulate(c, ready=False):
        previous = [jnp.zeros((8, LANES), f32)] * 8
        total = None if ready else [sums[8 * i : 8 * i + 8, :] for i in range(8)]
        for b in range(blocks + 1):
            spread(c, b, previous, ready)
            scan(b)
            collect(c, b, total)
        if not ready:
            for i, row in enumerate(total):
                sums[8 * i : 8 * i + 8, :] = row

    def edges(c):
        spread(c, 0, [jnp.zeros((8, LANES), f32)] * 8, True)
        spread(c, blocks, [turn(pbuf[c, 8 * i : 8 * i + 8, width - LANES : width]) for i in range(8)], True)
        for b in (0, blocks):
            scan(b)
            keep_edge(c, b, scanned(b))

    def increments(c):
        total = [late[8 * i : 8 * i + 8, :] for i in range(8)]
        for w in range(blocks):
            col = slice(w * LANES, (w + 1) * LANES)
            for i in range(8):
                at = slice(8 * i, 8 * i + 8)
                step = pbuf[c, at, col] + two_pi * wbuf[c, at, col].astype(f32)
                pbuf[c, at, col] = step
                total[i] = total[i] + step
        for i, row in enumerate(total):
            late[8 * i : 8 * i + 8, :] = row

    def arrived(c):
        for copy in load(c):
            copy.wait()

    def send_edges(c):
        @pl.when(chan > 0)
        def _():
            to_left(c).start()

        @pl.when(chan < n_chan - 1)
        def _():
            to_right(c).start()

    def send_ends(c):
        for_later(lambda d: ends_to(d, ends.at[c], ends_in.at[tm, c]).start())

    @pl.loop(0, cables - DEFER)
    def _(c):
        arrived(c)
        accumulate(c)

    pl.semaphore_wait(barrier, n_chan - 1 + n_tm - 1)

    pl.loop(0, cables - DEFER)(send_edges)
    pl.loop(0, EARLY)(send_ends)

    late[...] = jnp.zeros_like(late)

    @pl.loop(cables - DEFER, cables)
    def _(c):
        arrived(c)
        increments(c)
        edges(c)
        send_edges(c)

    for i in range(8):
        swap_in[0][pl.ds(25 * i, 8, stride=3), :] = late[8 * i : 8 * i + 8, :]
    scan(0)
    for i in range(8):
        sums[8 * i : 8 * i + 8, :] += swap_out[0][pl.ds(25 * i, 8, stride=3), :]

    both = jnp.concatenate([sums[...], jnp.zeros_like(sums)], axis=0)
    own_row[...] = jnp.sum(both.T, axis=0, keepdims=True)
    for_later(lambda d: row_to(d).start())
    pl.loop(EARLY, cables - DEFER)(send_ends)

    def to_plane(d):
        return pltpu.make_async_remote_copy(
            plane_row, plane_in.at[chan], s_plane, r_plane, device_id={"chan": chan ^ d}
        )

    def relay_row():
        from_earlier(lambda d: row_to(d).wait_recv())
        row = own_row[...]
        for source in range(n_tm - 1):
            last = row_in[source][:, times - 1 : times]
            row = row + jnp.where(source < tm, last, 0.0)
        plane_row[...] = row
        plane_in[chan] = row
        for d in sorted(range(1, n_chan), key=lambda d: -((d >> 4 & 1) + (d >> 2 & 1))):
            to_plane(d).start()

    def window(z, c, w):
        return jnp.concatenate(
            [jnp.concatenate([z[c, i, w], z[c, i, w + 1]], axis=1) for i in range(parts)],
            axis=0,
        )

    def push(c, register):
        for mxu in range(2):
            pltpu.matmul_push_rhs(matrix[c], register, mxu, transpose=True)

    def joined(acc):
        pair = pltpu.matmul_pop(acc)
        return pair[:, :LANES] + pair[:, LANES:]

    def filtered(first, acc, outer):
        order = [*range(1, blocks - 1)] + [0, blocks - 1] * outer
        work = [(first + k, w, n, k) for k in range(CABLES) for n, w in enumerate(order)]

        def finish(m):
            c, w, _, _ = work[m]
            ybuf[c, :, w * LANES : (w + 1) * LANES] = joined(acc[m % RING])

        push(first, 0)
        for m, (c, w, n, k) in enumerate(work):
            if m >= RING:
                finish(m - RING)
            fresh = k % 2 if n < 2 else None
            pltpu.matmul_acc_lhs(acc[m % RING], window(zhi, c, w), fresh)
            pltpu.matmul_acc_lhs(acc[m % RING], window(zlo, c, w))
            if n == 2 and k + 1 < CABLES:
                push(c + 1, (k + 1) % 2)
        for m in range(len(work) - RING, len(work)):
            finish(m)

    def all_plane():
        others = plane_in.at[pl.ds(0, n_chan - 1)]
        return pltpu.make_async_remote_copy(
            others, others, s_plane, r_plane, device_id={"chan": chan ^ 1}
        )

    def halos(c):
        @pl.when(chan > 0)
        def _():
            to_right(c).wait_recv()

        @pl.when(chan < n_chan - 1)
        def _():
            to_left(c).wait_recv()

    def relay_far():
        pl.loop(0, cables)(halos)
        last = slice(times // 2 - 1, times // 2)
        halo_rows = [halo[c, last, :] for halo in (halo_left, halo_right) for c in range(cables)]
        halo_rows = turn(jnp.concatenate(halo_rows, axis=0))
        from_left = lax.broadcasted_iota(jnp.int32, halo_rows.shape, 0) < cables
        low = lax.broadcasted_iota(jnp.int32, halo_rows.shape, 1) < LANES // 2
        far_send[...] = jnp.where(from_left == low, halo_rows, 0.0)
        for_later(lambda d: far_to(d).start())

    def edge_blocks(k):
        def tile(buffer, c, i):
            if buffer is send_left or buffer is send_right:
                return buffer[c, 8 * i : 8 * i + 8, :]
            packed = buffer[c, 8 * (i % 4) : 8 * (i % 4) + 8, :]
            return packed if i < 4 else turn(packed)

        for c in (k * CABLES + j for j in range(CABLES)):
            for at, low, high in ((0, halo_left, send_left), (blocks, send_right, halo_right)):
                put(c, at, [jnp.where(left, tile(low, c, i), tile(high, c, i)) for i in range(8)])

    def matmuls(body):
        pl.run_scoped(body, *[pltpu.ACC(n % 2)((times, 2 * LANES), f32) for n in range(RING)])

    @pl.loop(0, DEFER // CABLES)
    def _(k):
        pl.when(k == jnp.where(tm == 0, 0, RELAY))(relay_row)

        def body(*acc):
            filtered(k * CABLES, acc, False)
            for j in range(CABLES):
                accumulate(cables - DEFER + k * CABLES + j, ready=True)

        matmuls(body)
        for j in range(CABLES):
            send_ends(cables - DEFER + k * CABLES + j)

    relay_far()

    @pl.loop(DEFER // CABLES, cables // CABLES)
    def _(k):
        edge_blocks(k)
        matmuls(lambda *acc: filtered(k * CABLES, acc, True))

    from_earlier(lambda d: ends_to(d, ends, ends_in.at[tm]).wait_recv())
    from_earlier(lambda d: far_to(d).wait_recv())
    far = jnp.zeros_like(far_send)
    for source in range(n_tm - 1):
        far = far + jnp.where(source < tm, far_in[source], 0.0)

    position = lax.broadcasted_iota(jnp.int32, (blocks, LANES), 0)
    low_half = lax.broadcasted_iota(jnp.int32, (blocks, LANES), 1) < LANES // 2
    ones = jnp.ones((16, LANES), f32)
    which = lax.broadcasted_iota(jnp.int32, (16, LANES), 0)
    half = lax.broadcasted_iota(jnp.int32, (16, LANES), 1) < LANES // 2
    one_rows = jnp.concatenate(
        [
            jnp.where((which == 1) & half, 0.0, ones).astype(bf16),
            jnp.where((which == 2) & ~half, 0.0, ones).astype(bf16),
        ],
        axis=1,
    )

    for k in range(DEFER // CABLES):
        edge_blocks(k)

    def constants(*accs):
        outer = accs[2 * cables :]
        for c in range(cables):
            mxu, small, constant = c % 2, accs[2 * c], accs[2 * c + 1]
            own = jnp.zeros((blocks, LANES), f32)
            for source in range(n_tm - 1):
                own = own + jnp.where(source < tm, ends_in[source, c], 0.0)
            here = jnp.where((position == 0) & low_half, far[c : c + 1, :], own)
            after = jnp.where(
                (position == blocks - 1) & ~low_half,
                far[cables + c : cables + c + 1, :],
                pltpu.roll(own, blocks - 1, 0),
            )
            pltpu.matmul_push_rhs(matrix[c], 0, mxu, transpose=True)
            for i, pair in enumerate(zip(halves(here), halves(after))):
                pltpu.matmul_acc_lhs(small, jnp.concatenate(pair, axis=1), None if i else 0)
            pltpu.matmul_acc_lhs(constant, one_rows)
            if c < DEFER:
                for acc, w in zip(outer[2 * c :], (0, blocks - 1)):
                    pltpu.matmul_acc_lhs(acc, window(zhi, c, w))
                    pltpu.matmul_acc_lhs(acc, window(zlo, c, w))
        for c in range(cables):
            offset_out[c] = joined(accs[2 * c])
            if c < DEFER:
                for acc, w in zip(outer[2 * c :], (0, blocks - 1)):
                    ybuf[c, :, w * LANES : (w + 1) * LANES] = joined(acc)
            flat = joined(accs[2 * c + 1]) * coupling[c]
            edge = jnp.broadcast_to(flat[0:1, :], (blocks, LANES))
            edge = jnp.where((position == 0) & (chan == 0), flat[1:2, :], edge)
            edge = jnp.where((position == blocks - 1) & (chan == n_chan - 1), flat[2:3, :], edge)
            edge_out[c] = edge

    pl.run_scoped(
        constants,
        *[
            pltpu.ACC(c % 2)((size, 2 * LANES), f32)
            for c in range(cables)
            for size in (blocks, 16)
        ],
        *[pltpu.ACC(c % 2)((times, 2 * LANES), f32) for c in range(DEFER) for _ in range(2)],
    )

    for_later(lambda d: row_to(d).wait_send())
    for_later(lambda d: far_to(d).wait_send())
    for_later(lambda d: ends_to(d, ends, ends_in.at[tm]).wait_send())

    @pl.loop(0, cables)
    def _(c):
        @pl.when(chan > 0)
        def _():
            to_left(c).wait_send()

        @pl.when(chan < n_chan - 1)
        def _():
            to_right(c).wait_send()

    all_plane().wait_send()
    all_plane().wait_recv()
    row = jnp.sum(plane_in[...], axis=0) * (1.0 / (cables * blocks * LANES * n_chan))
    common_out[...] = jnp.broadcast_to(row, (LANES, LANES)).T[:times]


def final_kernel(y, offset, edge, common, out, buffer, sem):
    cables, _, width = y.shape

    def copy(c):
        return pltpu.make_async_copy(buffer.at[c], out.at[c], sem.at[c])

    @pl.loop(0, cables)
    def _(c):
        mode = common[...]
        for j in range(width // LANES):
            col = slice(j * LANES, (j + 1) * LANES)
            shift = offset[c, j : j + 1, :] - mode * edge[c, j : j + 1, :]
            buffer[c, :, col] = y[c, :, col] + shift
        copy(c).start()

    @pl.loop(0, cables)
    def _(c):
        copy(c).wait()


def shards(phase_step, wrap_count, coupling, filter_taps):
    cables, times, width = phase_step.shape
    blocks = width // LANES
    n_tm, n_chan = lax.axis_size("tm"), lax.axis_size("chan")
    vmem, dma = pltpu.VMEM, pltpu.SemaphoreType.DMA
    full = (cables, times, width)
    wide = (cables, times, width + LANES)
    edge = (cables + 1, times, LANES)
    z = (cables, times // 16, blocks + 1, 16, LANES)
    small = vmem((cables, blocks, LANES), f32)
    leveled = pl.pallas_call(
        functools.partial(main_kernel, n_tm, n_chan),
        out_shape=(
            vmem(full, f32),
            small,
            small,
            vmem((times, LANES), f32),
        ),
        in_specs=[
            pl.BlockSpec(memory_space=pl.ANY),
            pl.BlockSpec(memory_space=pl.ANY),
            pl.BlockSpec(memory_space=pltpu.SMEM),
            pl.BlockSpec(memory_space=vmem),
        ],
        out_specs=(
            pl.BlockSpec(memory_space=vmem),
            pl.BlockSpec(memory_space=vmem),
            pl.BlockSpec(memory_space=vmem),
            pl.BlockSpec(memory_space=vmem),
        ),
        scratch_shapes=[
            vmem(wide, f32), vmem(wide, jnp.int32), vmem(z, bf16), vmem(z, bf16),
            [vmem((200, LANES), f32)] * (blocks + 1), [vmem((200, LANES), f32)] * (blocks + 1),
            vmem((cables, 2 * LANES, 2 * LANES), bf16),
            vmem((times, LANES), f32), vmem((times, LANES), f32), vmem((cables, blocks, LANES), f32),
            vmem(edge, f32), vmem(edge, f32),
            *[vmem((cables, times // 2, LANES), f32)] * 4,
            vmem((n_tm, cables, blocks, LANES), f32),
            vmem((2 * cables, LANES), f32), vmem((n_tm, 2 * cables, LANES), f32),
            vmem((1, LANES), f32), vmem((n_tm, 1, LANES), f32),
            vmem((1, LANES), f32), vmem((n_chan, 1, LANES), f32),
            dma((2, cables)), dma((cables,)), dma((cables,)), dma((cables,)), dma((cables,)),
            dma((n_tm - 1,)), dma((n_tm - 1,)),
            dma((n_tm - 1,)), dma((n_tm - 1,)),
            dma((n_tm - 1,)), dma((n_tm - 1,)),
            dma, dma,
        ],
        compiler_params=pltpu.CompilerParams(
            collective_id=0, has_side_effects=True, vmem_limit_bytes=LIMIT << 20
        ),
        name="level",
    )(phase_step, wrap_count, coupling, filter_taps)
    return pl.pallas_call(
        final_kernel,
        out_shape=jax.ShapeDtypeStruct(full, f32),
        in_specs=[pl.BlockSpec(memory_space=vmem)] * 4,
        out_specs=pl.BlockSpec(memory_space=pl.ANY),
        scratch_shapes=[vmem(full, f32), dma((cables,))],
        compiler_params=pltpu.CompilerParams(vmem_limit_bytes=16 << 20),
        name="finish",
    )(*[pltpu.with_memory_space_constraint(x, vmem) for x in leveled])


def solution(mesh):
    placed = (P(None, "tm", "chan"), P(None, "tm", "chan"), P(), P())
    return jax.shard_map(
        shards, mesh=mesh, in_specs=placed, out_specs=P(None, "tm", "chan"), check_vma=False
    )
```
